768 devices in a mesh: section: 32 (over x, z_hi, core), tensor: 24 (over y, z_lo).
Axes of the slice: x: 4, y: 8, z: 12 (z_hi: 4, z_lo: 3; z = z_hi * 3 + z_lo), core: 2. Of those that a mesh axis runs over, the one named last changes fastest.
Arguments:
- fwd_input: bfloat16 [32, 64, 4608], P('section', None, 'tensor'), may hold values from -6 to 6
- bwd_grad: bfloat16 [32, 64, 4608], P('section', None, 'tensor'), may hold values from -6 to 6
- parked: bfloat16 [32, 64, 4608], P('section', None, 'tensor'), may hold values from -6 to 6
- norm_gain: float32 [32, 4608], P('section'), may hold values from 0.25 to 1.75
- w_query: bfloat16 [32, 4608, 3072], P('section', None, 'tensor'), may hold values from -1 to 1
- w_key: bfloat16 [32, 4608, 3072], P('section', None, 'tensor'), may hold values from -1 to 1
- w_value: bfloat16 [32, 4608, 3072], P('section', None, 'tensor'), may hold values from -0.09375 to 0.09375
- w_out: bfloat16 [32, 3072, 4608], P('section', 'tensor'), may hold values from -0.109375 to 0.109375
- offsets: int32 [32, 2, 8], P('section'), may hold values from 0 to 56, as said below
- mirror: int32 [32], replicated, may hold values from 0 to 31, as said below
Outputs:
- next_input: bfloat16 [32, 64, 4608], P('section', None, 'tensor')
- prev_grad: bfloat16 [32, 64, 4608], P('section', None, 'tensor')
- parked_new: bfloat16 [32, 64, 4608], P('section', None, 'tensor')
The draws below stay inside these ranges and needn't reach their ends.
Inputs may be any that keep to these rules, and one draw needn't show every extreme that they name: Each row offsets[s, j] holds the numbers 0, 8, ..., 56 once each. mirror[t] = t XOR m for one m with 32 / 2 <= m < 32, so sections of the first half pair with sections of the second half.
All inputs are finite; a program needn't handle non-finite values.
Results may differ from the reference program's by a relative error of at most 0.018.
Values may be sent and summed in bfloat16 or wider, within the bound.
No kernel may reach another device: no remote copies, remote signals or barrier semaphores. Data moves between devices by JAX's collectives and lax.ppermute only.
A program may use at most 32 MiB of HBM per device.

```python
import math
import jax
import jax.numpy as jnp
from jax import lax

DW = 4608
HD = 64
HEADS_DEV = 2
HEADS = 48
SPAN = 8
NCH = 8
ROWS = 64
N_SECTION = 32
N_TENSOR = 24


def projection_draw(key, salt):
    scale = DW ** (-0.5)
    salted = jax.random.fold_in(key, salt)

    def one_section(section):
        noise = jax.random.truncated_normal(jax.random.fold_in(salted, section), -6.0, 6.0, (DW, HEADS * HD), jnp.float32) * scale
        return noise
    return lax.map(one_section, jnp.arange(N_SECTION, dtype=jnp.int32)).astype(jnp.bfloat16)


def activation_draw(key, salt):
    salted = jax.random.fold_in(key, salt)

    def one_section(section):
        section_key = jax.random.fold_in(salted, section)
        rows = jax.random.truncated_normal(section_key, -6.0, 6.0, (ROWS, DW), jnp.float32)
        return jnp.clip(rows, -6.0, 6.0)
    return lax.map(one_section, jnp.arange(N_SECTION, dtype=jnp.int32)).astype(jnp.bfloat16)


def draw_w_query(key, part):
    return projection_draw(key, 31)


def draw_w_key(key, part):
    return projection_draw(key, 37)


def draw_fwd_input(key, part):
    return activation_draw(key, 41)


def draw_parked(key, part):
    return activation_draw(key, 43)


def draw_offsets(key, part):
    row_keys = jax.random.split(jax.random.fold_in(key, 11), N_SECTION * 2)
    orders = jax.vmap(lambda row_key: jax.random.permutation(row_key, NCH))(row_keys)
    return (orders.reshape(N_SECTION, 2, NCH) * SPAN).astype(jnp.int32)


def draw_mirror(key, part):
    xor_mask = jax.random.randint(jax.random.fold_in(key, 23), (), N_SECTION // 2, N_SECTION)
    return jnp.bitwise_xor(jnp.arange(N_SECTION, dtype=jnp.int32), xor_mask.astype(jnp.int32)).astype(jnp.int32)


def block_scale(key, dims, pieces, least, largest):
    gain, own = 1.0, jax.random.fold_in(key, 6)
    for axis_at, parts in pieces:
        heights = jnp.exp(jax.random.uniform(jax.random.fold_in(own, axis_at), (parts,), jnp.float32, least / len(pieces), largest / len(pieces)))
        gain = gain * jnp.repeat(heights, dims[axis_at] // parts).reshape([-1 if axis == axis_at else 1 for axis in range(len(dims))])
    return gain


def normal_values(own_key, shape, width, most, shards=(), held_as=jnp.bfloat16):
    result = jax.random.normal(own_key, shape, jnp.float32) * width
    if len(shards) > 0:
        result = block_scale(own_key, shape, shards, -0.22, 0.18) * result
    return jnp.clip(result, min=-most, max=most).astype(held_as)


def setup_inputs(seed: int = 0) -> dict:
    key_of = jax.random.split(jax.random.key(seed), 11)
    return {
        "fwd_input": draw_fwd_input(jax.random.fold_in(key_of[10], 71), 0),
        "bwd_grad": normal_values(key_of[1], (N_SECTION, ROWS, DW), 1.0, 6.0, ((0, 32), (2, 24))),
        "parked": draw_parked(jax.random.fold_in(key_of[10], 71), 0),
        "norm_gain": jnp.clip(1.0 + 0.15 * jax.random.normal(key_of[3], (N_SECTION, DW), jnp.float32), 0.25, 1.75),
        "w_query": draw_w_query(jax.random.fold_in(key_of[10], 71), 0),
        "w_key": draw_w_key(jax.random.fold_in(key_of[10], 71), 0),
        "w_value": normal_values(key_of[6], (N_SECTION, DW, HEADS * HD), DW ** -0.5, 0.09375, ((0, 32), (2, 24))),
        "w_out": normal_values(key_of[7], (N_SECTION, HEADS * HD, DW), (HEADS * HD) ** -0.5, 0.109375, ((0, 32), (1, 24))),
        "offsets": draw_offsets(jax.random.fold_in(key_of[10], 71), 0),
        "mirror": draw_mirror(jax.random.fold_in(key_of[10], 71), 0),
    }


def token_positions(starts, row_count):
    rows_iota = jnp.arange(row_count, dtype=jnp.int32)
    block_id = rows_iota // SPAN
    chosen = block_id[:, None] == jnp.arange(starts.shape[0], dtype=jnp.int32)[None, :]
    return lax.optimization_barrier(jnp.sum(jnp.where(chosen, starts[None, :], 0), axis=1)).astype(jnp.int32) + rows_iota % SPAN

def branch(inputs, norm_scale, query_part, key_part, value_part, out_part, places):
    row_count = inputs.shape[0]
    head_count = query_part.shape[1] // HD
    widened = inputs.astype(jnp.float32)
    inverse = lax.rsqrt(lax.optimization_barrier(jnp.mean(widened * widened, axis=1, keepdims=True)) + 1e-05)
    normed = (widened * inverse * norm_scale[None, :]).astype(jnp.bfloat16)
    queries = jnp.dot(normed, query_part, preferred_element_type=jnp.float32).astype(jnp.bfloat16).reshape(row_count, head_count, HD)
    key_rows = jnp.dot(normed, key_part, preferred_element_type=jnp.float32).astype(jnp.bfloat16).reshape(row_count, head_count, HD)
    value_rows = jnp.dot(normed, value_part, preferred_element_type=jnp.float32).astype(jnp.bfloat16).reshape(row_count, head_count, HD)
    scores = jnp.einsum('qhd,khd->hqk', queries.astype(jnp.float32), key_rows.astype(jnp.float32)) / math.sqrt(HD)
    allowed = places[None, :, None] >= places[None, None, :]
    scores = jnp.where(allowed, scores, -1e+30)
    row_max = lax.optimization_barrier(jnp.max(scores, axis=2, keepdims=True))
    exp_scores = jnp.exp(scores - row_max)
    weights = (exp_scores / lax.optimization_barrier(jnp.sum(exp_scores, axis=2, keepdims=True))).astype(jnp.bfloat16)
    context = jnp.einsum('hqk,khd->qhd', weights.astype(jnp.float32), value_rows.astype(jnp.float32)).astype(jnp.bfloat16)
    return jnp.dot(context.reshape(row_count, head_count * HD), out_part, preferred_element_type=jnp.float32)

def rounded(term):
    return lax.optimization_barrier(term.astype(jnp.bfloat16)).astype(jnp.float32)

def reference(fwd_input, bwd_grad, parked, norm_gain, w_query, w_key, w_value, w_out, offsets, mirror):
    group_width = HEADS_DEV * HD
    fetched = jnp.take(parked, mirror, axis=0)

    def one_section(section_index):
        fwd_rows = fwd_input[section_index]
        grad_rows = bwd_grad[section_index]
        stashed = fetched[section_index]
        scale_row = norm_gain[section_index]
        pos_fwd = token_positions(offsets[section_index, 0], ROWS)
        pos_bwd = token_positions(offsets[section_index, 1], ROWS)

        def one_group(group):
            first_col = (group * group_width).astype(jnp.int32)
            query_part = lax.dynamic_slice_in_dim(w_query[section_index], first_col, group_width, 1)
            key_part = lax.dynamic_slice_in_dim(w_key[section_index], first_col, group_width, 1)
            value_part = lax.dynamic_slice_in_dim(w_value[section_index], first_col, group_width, 1)
            out_part = lax.dynamic_slice_in_dim(w_out[section_index], first_col, group_width, 0)
            forward_term = branch(fwd_rows, scale_row, query_part, key_part, value_part, out_part, pos_fwd)

            def stashed_branch(layer_in):
                return branch(layer_in, scale_row, query_part, key_part, value_part, out_part, pos_bwd)
            unused, pullback = jax.vjp(stashed_branch, stashed)
            back_term, = pullback(grad_rows.astype(jnp.float32))
            return (rounded(forward_term), rounded(back_term.astype(jnp.float32)))
        forward_parts, back_parts = lax.map(one_group, jnp.arange(N_TENSOR, dtype=jnp.int32))
        layer_out = (fwd_rows.astype(jnp.float32) + lax.optimization_barrier(jnp.sum(forward_parts, axis=0))).astype(jnp.bfloat16)
        grad_out = (grad_rows.astype(jnp.float32) + lax.optimization_barrier(jnp.sum(back_parts, axis=0))).astype(jnp.bfloat16)
        return (layer_out, grad_out)
    layer_outs, grad_outs = lax.map(one_section, jnp.arange(N_SECTION, dtype=jnp.int32))
    zero_block = jnp.zeros_like(layer_outs[:1])
    next_input = jnp.concatenate([zero_block, layer_outs[:-1]], axis=0)
    prev_grad = jnp.concatenate([grad_outs[1:], zero_block], axis=0)
    parked_new = jnp.take(fwd_input, mirror, axis=0)
    return (next_input, prev_grad, parked_new)
```

```python
import math

import jax
import jax.numpy as jnp
from jax import lax
from jax.sharding import PartitionSpec as P

HD = 64
SPAN = 8


def passed_along(block, axis, distance):
    devices = range(lax.axis_size(axis))
    route = [(i - distance, i) for i in devices if i - distance in devices]
    return lax.ppermute(block, axis, route)


def token_positions(starts, row_count):
    rows_iota = jnp.arange(row_count, dtype=jnp.int32)
    block_id = rows_iota // SPAN
    chosen = block_id[:, None] == jnp.arange(starts.shape[0], dtype=jnp.int32)[None, :]
    return jnp.sum(jnp.where(chosen, starts[None, :], 0), axis=1) + rows_iota % SPAN


def branch(inputs, norm_scale, query_part, key_part, value_part, out_part, places):
    row_count = inputs.shape[0]
    head_count = query_part.shape[1] // HD
    widened = inputs.astype(jnp.float32)
    inverse = lax.rsqrt(jnp.mean(widened * widened, axis=1, keepdims=True) + 1e-05)
    normed = (widened * inverse * norm_scale[None, :]).astype(jnp.bfloat16)
    queries = (
        jnp.dot(normed, query_part, preferred_element_type=jnp.float32)
        .astype(jnp.bfloat16)
        .reshape(row_count, head_count, HD)
    )
    key_rows = (
        jnp.dot(normed, key_part, preferred_element_type=jnp.float32)
        .astype(jnp.bfloat16)
        .reshape(row_count, head_count, HD)
    )
    value_rows = (
        jnp.dot(normed, value_part, preferred_element_type=jnp.float32)
        .astype(jnp.bfloat16)
        .reshape(row_count, head_count, HD)
    )
    scores = jnp.einsum(
        "qhd,khd->hqk", queries.astype(jnp.float32), key_rows.astype(jnp.float32)
    ) / math.sqrt(HD)
    allowed = places[None, :, None] >= places[None, None, :]
    scores = jnp.where(allowed, scores, -1e30)
    row_max = jnp.max(scores, axis=2, keepdims=True)
    exp_scores = jnp.exp(scores - row_max)
    weights = (exp_scores / jnp.sum(exp_scores, axis=2, keepdims=True)).astype(jnp.bfloat16)
    context = jnp.einsum(
        "hqk,khd->qhd", weights.astype(jnp.float32), value_rows.astype(jnp.float32)
    ).astype(jnp.bfloat16)
    return jnp.dot(
        context.reshape(row_count, head_count * HD), out_part, preferred_element_type=jnp.float32
    )


def mirrored(values, mask):
    section_count = lax.axis_size("section")
    half = section_count // 2

    def swap_by(distance):
        route = [(i, i ^ distance) for i in range(section_count)]
        return lambda held: lax.ppermute(held, "section", route)

    return lax.switch(mask - half, [swap_by(half + i) for i in range(half)], values)


def exchanged(blocks):
    return lax.all_to_all(blocks, "tensor", 0, 0, tiled=True)


def spread(block):
    return exchanged(jnp.broadcast_to(block[None], (lax.axis_size("tensor"),) + block.shape))


def side_by_side(blocks):
    return blocks.transpose(1, 0, 2).reshape(blocks.shape[1], -1)


def by_device(whole):
    parts = lax.axis_size("tensor")
    return whole.reshape(whole.shape[0], parts, -1).transpose(1, 0, 2)


def local(fwd_input, bwd_grad, parked, norm_gain, w_query, w_key, w_value, w_out, offsets, mirror):
    fwd_rows = fwd_input[0]
    grad_rows = bwd_grad[0]
    share = fwd_rows.shape[1]
    swapped = mirrored(jnp.concatenate([fwd_rows, parked[0]], axis=1), mirror[0])
    parked_rows = swapped[:, :share]
    fetched = swapped[:, share:]
    pair = spread(jnp.concatenate([fwd_rows, grad_rows, fetched], axis=1))
    full_fwd = side_by_side(pair[:, :, :share])
    full_grad = side_by_side(pair[:, :, share : 2 * share])
    full_back = side_by_side(pair[:, :, 2 * share : 3 * share])
    scale_row = norm_gain[0]
    pos_fwd = token_positions(offsets[0, 0], full_fwd.shape[0])
    pos_bwd = token_positions(offsets[0, 1], full_back.shape[0])
    query_part = w_query[0]
    key_part = w_key[0]
    value_part = w_value[0]
    out_part = w_out[0]
    forward_term = branch(full_fwd, scale_row, query_part, key_part, value_part, out_part, pos_fwd)

    def stashed_branch(layer_in):
        return branch(layer_in, scale_row, query_part, key_part, value_part, out_part, pos_bwd)

    unused, pullback = jax.vjp(stashed_branch, full_back)
    (back_term,) = pullback(full_grad.astype(jnp.float32))
    terms = jnp.concatenate(
        [by_device(forward_term.astype(jnp.bfloat16)), by_device(back_term.astype(jnp.bfloat16))], axis=2
    )
    sums = jnp.sum(exchanged(terms).astype(jnp.float32), axis=0)
    layer_out = (fwd_rows.astype(jnp.float32) + sums[:, :share]).astype(jnp.bfloat16)
    grad_out = (grad_rows.astype(jnp.float32) + sums[:, share:]).astype(jnp.bfloat16)
    next_rows = passed_along(layer_out, "section", 1)
    prev_rows = passed_along(grad_out, "section", -1)
    return (next_rows[None], prev_rows[None], parked_rows[None])


def solution(mesh):
    in_specs = (
        P("section", None, "tensor"),
        P("section", None, "tensor"),
        P("section", None, "tensor"),
        P("section", None),
        P("section", None, "tensor"),
        P("section", None, "tensor"),
        P("section", None, "tensor"),
        P("section", "tensor", None),
        P("section", None, None),
        P(),
    )
    out_specs = (
        P("section", None, "tensor"),
        P("section", None, "tensor"),
        P("section", None, "tensor"),
    )
    return jax.shard_map(local, mesh=mesh, in_specs=in_specs, out_specs=out_specs, check_vma=False)
```

```python
import math

import jax
import jax.numpy as jnp
from jax import lax
from jax.experimental import pallas as pl
from jax.experimental.pallas import tpu as pltpu
from jax.sharding import PartitionSpec as P

HD = 64
EPS = 1e-05
F32 = jnp.float32
BF16 = jnp.bfloat16


def dot(a, b):
    return jnp.dot(a, b, preferred_element_type=F32)


def dot_t(a, b):
    return lax.dot_general(a, b, (((1,), (1,)), ((), ())), preferred_element_type=F32)


def dot_tl(a, b):
    return lax.dot_general(a, b, (((0,), (0,)), ((), ())), preferred_element_type=F32)


def causal(off_ref, which, rows):
    row = lax.broadcasted_iota(jnp.int32, (rows, rows), 0)
    col = lax.broadcasted_iota(jnp.int32, (rows, rows), 1)
    row_start = jnp.zeros((rows, rows), jnp.int32)
    col_start = jnp.zeros((rows, rows), jnp.int32)
    for c in range(off_ref.shape[2]):
        start = off_ref[0, which, c]
        row_start = jnp.where((row >> 3) == c, start, row_start)
        col_start = jnp.where((col >> 3) == c, start, col_start)
    return row_start + (row & 7) >= col_start + (col & 7)


def softmax(queries, keys, mask):
    scores = dot_t(queries, keys) * (1.0 / math.sqrt(HD))
    scores = jnp.where(mask, scores, -1e30)
    top = jnp.max(scores, axis=1, keepdims=True)
    grown = jnp.exp(scores - top)
    return grown / jnp.sum(grown, axis=1, keepdims=True)


def heads_of(*arrays):
    count = arrays[0].shape[1] // HD
    return [tuple(a[:, h * HD : (h + 1) * HD] for a in arrays) for h in range(count)]


def forward_kernel(off_ref, pair_ref, gain_ref, wq_ref, wk_ref, wv_ref, wo_ref, term_ref, dctx_ref, xs, gs):
    parts, rows, wide = pair_ref.shape
    share = wide // 2
    half = rows // 2
    width = parts * share
    squares = jnp.zeros((rows, wide), F32)
    for u in range(parts // 2):
        a = pair_ref[2 * u]
        b = pair_ref[2 * u + 1]
        span = slice(wide * u, wide * (u + 1))
        x = jnp.concatenate([a[:, :share], b[:, :share]], axis=1)
        xs[:, span] = x
        gs[:, span] = jnp.concatenate([a[:, share:], b[:, share:]], axis=1)
        x = x.astype(F32)
        squares = squares + x * x
    inverse = lax.rsqrt(jnp.sum(squares, axis=1, keepdims=True) * (1.0 / width) + EPS)
    for u in range(parts // 2):
        span = slice(wide * u, wide * (u + 1))
        xs[:, span] = (xs[:, span].astype(F32) * inverse * gain_ref[:, span]).astype(BF16)
    normed = xs[...]
    queries = dot(normed, wq_ref[...]).astype(BF16)
    keys = dot(normed, wk_ref[...]).astype(BF16)
    values = dot(normed, wv_ref[...]).astype(BF16)
    mask = causal(off_ref, 0, rows)
    context = jnp.concatenate(
        [dot(softmax(q, k, mask).astype(BF16), v) for q, k, v in heads_of(queries, keys, values)], axis=1
    ).astype(BF16)
    for u in range(parts // 2):
        span = slice(wide * u, wide * (u + 1))
        out = dot(context, wo_ref[:, span]).astype(BF16)
        term_ref[2 * u] = jnp.concatenate([out[:half, :share], out[half:, :share]], axis=1)
        term_ref[2 * u + 1] = jnp.concatenate([out[:half, share:], out[half:, share:]], axis=1)
    dctx_ref[...] = dot_t(gs[...], wo_ref[...]).astype(BF16)


def backward_kernel(off_ref, back_ref, dctx_ref, gain_ref, wq_ref, wk_ref, wv_ref, term_ref, xs, ns, ds):
    parts, half, wide = back_ref.shape
    share = wide // 2
    rows = half * 2
    width = parts * share
    squares = jnp.zeros((rows, wide), F32)
    for u in range(parts // 2):
        a = back_ref[2 * u]
        b = back_ref[2 * u + 1]
        span = slice(wide * u, wide * (u + 1))
        x = jnp.concatenate(
            [
                jnp.concatenate([a[:, :share], b[:, :share]], axis=1),
                jnp.concatenate([a[:, share:], b[:, share:]], axis=1),
            ],
            axis=0,
        )
        xs[:, span] = x
        x = x.astype(F32)
        squares = squares + x * x
    inverse = lax.rsqrt(jnp.sum(squares, axis=1, keepdims=True) * (1.0 / width) + EPS)
    for u in range(parts // 2):
        span = slice(wide * u, wide * (u + 1))
        ns[:, span] = (xs[:, span].astype(F32) * inverse * gain_ref[:, span]).astype(BF16)
    normed = ns[...]
    queries = dot(normed, wq_ref[...]).astype(BF16)
    keys = dot(normed, wk_ref[...]).astype(BF16)
    values = dot(normed, wv_ref[...]).astype(BF16)
    mask = causal(off_ref, 1, rows)
    grads = []
    for q, k, v, dc in heads_of(queries, keys, values, dctx_ref[...]):
        weights = softmax(q, k, mask)
        dvalue = dot_tl(weights.astype(BF16), dc)
        dweights = dot_t(dc, v).astype(BF16).astype(F32)
        dscores = weights * (dweights - jnp.sum(dweights * weights, axis=1, keepdims=True))
        dscores = jnp.where(mask, dscores, 0.0) * (1.0 / math.sqrt(HD))
        dscores = dscores.astype(BF16)
        grads.append((dot(dscores, k), dot_tl(dscores, q), dvalue))
    dq, dk, dv = (jnp.concatenate(g, axis=1).astype(BF16) for g in zip(*grads))
    along = jnp.zeros((rows, wide), F32)
    for u in range(parts // 2):
        span = slice(wide * u, wide * (u + 1))
        grown = dot_t(dq, wq_ref[span, :]) + dot_t(dk, wk_ref[span, :]) + dot_t(dv, wv_ref[span, :])
        grown = grown * gain_ref[:, span]
        ds[:, span] = grown
        along = along + grown * xs[:, span].astype(F32)
    factor = jnp.sum(along, axis=1, keepdims=True) * (inverse * inverse * inverse) * (1.0 / width)
    for u in range(parts // 2):
        span = slice(wide * u, wide * (u + 1))
        out = (ds[:, span] * inverse - xs[:, span].astype(F32) * factor).astype(BF16)
        term_ref[2 * u] = jnp.concatenate([out[:half, :share], out[half:, :share]], axis=1)
        term_ref[2 * u + 1] = jnp.concatenate([out[:half, share:], out[half:, share:]], axis=1)


def kernel_call(body, outs, scratch, args):
    vmem = pl.BlockSpec(memory_space=pltpu.VMEM)
    specs = [pl.BlockSpec(memory_space=pltpu.SMEM)] + [vmem] * (len(args) - 1)
    return pl.pallas_call(
        body,
        out_shape=outs,
        in_specs=specs,
        out_specs=jax.tree.map(lambda _: vmem, outs),
        scratch_shapes=scratch,
        compiler_params=pltpu.CompilerParams(vmem_limit_bytes=VMEM_LIMIT),
    )(*args)


VMEM_LIMIT = 24 * 2**20


def forward_term(offsets, pair, gain, wq, wk, wv, wo):
    parts, rows, wide = pair.shape
    width = gain.shape[1]
    outs = (
        jax.ShapeDtypeStruct((parts, rows // 2, wide), BF16),
        jax.ShapeDtypeStruct((rows, wo.shape[0]), BF16),
    )
    scratch = [pltpu.VMEM((rows, width), BF16), pltpu.VMEM((rows, width), BF16)]
    return kernel_call(forward_kernel, outs, scratch, (offsets, pair, gain, wq, wk, wv, wo))


def backward_term(offsets, back, dctx, gain, wq, wk, wv):
    _, half, _ = back.shape
    width = gain.shape[1]
    outs = jax.ShapeDtypeStruct(back.shape, BF16)
    scratch = [
        pltpu.VMEM((2 * half, width), BF16),
        pltpu.VMEM((2 * half, width), BF16),
        pltpu.VMEM((2 * half, width), F32),
    ]
    return kernel_call(backward_kernel, outs, scratch, (offsets, back, dctx, gain, wq, wk, wv))


def folded(block):
    half = block.shape[0] // 2
    return jnp.concatenate([block[:half], block[half:]], axis=1)


def unfolded(block):
    share = block.shape[1] // 2
    return jnp.concatenate([block[:, :share], block[:, share:]], axis=0)


def passed_along(block, axis, distance):
    devices = range(lax.axis_size(axis))
    route = [(i - distance, i) for i in devices if i - distance in devices]
    return lax.ppermute(block, axis, route)


def mirrored(values, mask):
    section_count = lax.axis_size("section")
    half = section_count // 2

    def swap_by(distance):
        route = [(i, i ^ distance) for i in range(section_count)]
        return lambda held: lax.ppermute(held, "section", route)

    return lax.switch(mask - half, [swap_by(half + i) for i in range(half)], values)


def exchanged(blocks):
    return lax.all_to_all(blocks, "tensor", 0, 0, tiled=True)


def spread(block):
    return exchanged(jnp.broadcast_to(block[None], (lax.axis_size("tensor"),) + block.shape))


def total(rows, terms):
    summed = jnp.sum(exchanged(terms).astype(F32), axis=0)
    return unfolded((folded(rows).astype(F32) + summed).astype(BF16))


def local(fwd_input, bwd_grad, parked, norm_gain, w_query, w_key, w_value, w_out, offsets, mirror):
    fwd_rows = fwd_input[0]
    grad_rows = bwd_grad[0]
    half = fwd_rows.shape[0] // 2
    pair = spread(jnp.concatenate([fwd_rows, grad_rows], axis=1))
    swapped = mirrored(jnp.concatenate([folded(fwd_rows), folded(parked[0])], axis=0), mirror[0])
    back = spread(swapped[half:])
    parked_rows = unfolded(swapped[:half])
    term, dctx = forward_term(offsets, pair, norm_gain, w_query[0], w_key[0], w_value[0], w_out[0])
    layer_out = total(fwd_rows, term)
    next_rows = passed_along(layer_out, "section", 1)
    back_term = backward_term(offsets, back, dctx, norm_gain, w_query[0], w_key[0], w_value[0])
    grad_out = total(grad_rows, back_term)
    prev_rows = passed_along(grad_out, "section", -1)
    return (next_rows[None], prev_rows[None], parked_rows[None])


def solution(mesh):
    in_specs = (
        P("section", None, "tensor"),
        P("section", None, "tensor"),
        P("section", None, "tensor"),
        P("section", None),
        P("section", None, "tensor"),
        P("section", None, "tensor"),
        P("section", None, "tensor"),
        P("section", "tensor", None),
        P("section", None, None),
        P(),
    )
    out_specs = (
        P("section", None, "tensor"),
        P("section", None, "tensor"),
        P("section", None, "tensor"),
    )
    return jax.shard_map(local, mesh=mesh, in_specs=in_specs, out_specs=out_specs, check_vma=False)
```

```python
import math

import jax
import jax.numpy as jnp
from jax import lax
from jax.experimental import pallas as pl
from jax.experimental.pallas import tpu as pltpu
from jax.sharding import Mesh
from jax.sharding import PartitionSpec as P

HD = 64
EPS = 1e-05
F32 = jnp.float32
BF16 = jnp.bfloat16


def dot(a, b):
    return jnp.dot(a, b, preferred_element_type=F32)


def dot_t(a, b):
    return lax.dot_general(a, b, (((1,), (1,)), ((), ())), preferred_element_type=F32)


def dot_tl(a, b):
    return lax.dot_general(a, b, (((0,), (0,)), ((), ())), preferred_element_type=F32)


def causal(off_ref, which, rows):
    row = lax.broadcasted_iota(jnp.int32, (rows, rows), 0)
    col = lax.broadcasted_iota(jnp.int32, (rows, rows), 1)
    row_start = jnp.zeros((rows, rows), jnp.int32)
    col_start = jnp.zeros((rows, rows), jnp.int32)
    for c in range(off_ref.shape[2]):
        start = off_ref[0, which, c]
        row_start = jnp.where((row >> 3) == c, start, row_start)
        col_start = jnp.where((col >> 3) == c, start, col_start)
    return row_start + (row & 7) >= col_start + (col & 7)


def softmax(queries, keys, mask):
    scores = dot_t(queries, keys) * (1.0 / math.sqrt(HD))
    scores = jnp.where(mask, scores, -1e30)
    top = jnp.max(scores, axis=1, keepdims=True)
    grown = jnp.exp(scores - top)
    return grown / jnp.sum(grown, axis=1, keepdims=True)


def heads_of(*arrays):
    count = arrays[0].shape[1] // HD
    return [tuple(a[:, h * HD : (h + 1) * HD] for a in arrays) for h in range(count)]


def gathered(own_ref, low_ref, high_ref, all_ref):
    count = all_ref.shape[0]
    at = lax.axis_index("run")
    all_ref[at] = own_ref[...]
    all_ref[lax.rem(at + count - 1, count)] = low_ref[...]
    all_ref[lax.rem(at + 1, count)] = high_ref[...]


def forward_kernel(
    off_ref, own_ref, low_ref, high_ref, gain_ref, wq_ref, wk_ref, wv_ref, wo_ref, term_ref, dctx_ref, blocks, xs, gs
):
    gathered(own_ref, low_ref, high_ref, blocks)
    runs, lines, rows, wide = blocks.shape
    parts = runs * lines
    share = wide // 2
    half = rows // 2
    width = parts * share
    squares = jnp.zeros((rows, wide), F32)
    for u in range(parts // 2):
        a = blocks[(2 * u) % runs, (2 * u) // runs]
        b = blocks[(2 * u + 1) % runs, (2 * u + 1) // runs]
        span = slice(wide * u, wide * (u + 1))
        x = jnp.concatenate([a[:, :share], b[:, :share]], axis=1)
        xs[:, span] = x
        gs[:, span] = jnp.concatenate([a[:, share:], b[:, share:]], axis=1)
        x = x.astype(F32)
        squares = squares + x * x
    inverse = lax.rsqrt(jnp.sum(squares, axis=1, keepdims=True) * (1.0 / width) + EPS)
    for u in range(parts // 2):
        span = slice(wide * u, wide * (u + 1))
        xs[:, span] = (xs[:, span].astype(F32) * inverse * gain_ref[:, span]).astype(BF16)
    normed = xs[...]
    queries = dot(normed, wq_ref[...]).astype(BF16)
    keys = dot(normed, wk_ref[...]).astype(BF16)
    values = dot(normed, wv_ref[...]).astype(BF16)
    mask = causal(off_ref, 0, rows)
    context = jnp.concatenate(
        [dot(softmax(q, k, mask).astype(BF16), v) for q, k, v in heads_of(queries, keys, values)], axis=1
    ).astype(BF16)
    for u in range(parts // 2):
        span = slice(wide * u, wide * (u + 1))
        out = dot(context, wo_ref[:, span]).astype(BF16)
        term_ref[2 * u] = jnp.concatenate([out[:half, :share], out[half:, :share]], axis=1)
        term_ref[2 * u + 1] = jnp.concatenate([out[:half, share:], out[half:, share:]], axis=1)
    dctx_ref[...] = dot_t(gs[...], wo_ref[...]).astype(BF16)


def backward_kernel(
    off_ref,
    own_ref,
    low_ref,
    high_ref,
    dctx_ref,
    gain_ref,
    wq_ref,
    wk_ref,
    wv_ref,
    stay_ref,
    up_ref,
    down_ref,
    blocks,
    terms,
    xs,
    ns,
    ds,
):
    gathered(own_ref, low_ref, high_ref, blocks)
    runs, lines, half, wide = blocks.shape
    parts = runs * lines
    share = wide // 2
    rows = half * 2
    width = parts * share
    squares = jnp.zeros((rows, wide), F32)
    for u in range(parts // 2):
        a = blocks[(2 * u) % runs, (2 * u) // runs]
        b = blocks[(2 * u + 1) % runs, (2 * u + 1) // runs]
        span = slice(wide * u, wide * (u + 1))
        x = jnp.concatenate(
            [
                jnp.concatenate([a[:, :share], b[:, :share]], axis=1),
                jnp.concatenate([a[:, share:], b[:, share:]], axis=1),
            ],
            axis=0,
        )
        xs[:, span] = x
        x = x.astype(F32)
        squares = squares + x * x
    inverse = lax.rsqrt(jnp.sum(squares, axis=1, keepdims=True) * (1.0 / width) + EPS)
    for u in range(parts // 2):
        span = slice(wide * u, wide * (u + 1))
        ns[:, span] = (xs[:, span].astype(F32) * inverse * gain_ref[:, span]).astype(BF16)
    normed = ns[...]
    queries = dot(normed, wq_ref[...]).astype(BF16)
    keys = dot(normed, wk_ref[...]).astype(BF16)
    values = dot(normed, wv_ref[...]).astype(BF16)
    mask = causal(off_ref, 1, rows)
    grads = []
    for q, k, v, dc in heads_of(queries, keys, values, dctx_ref[...]):
        weights = softmax(q, k, mask)
        dvalue = dot_tl(weights.astype(BF16), dc)
        dweights = dot_t(dc, v).astype(BF16).astype(F32)
        dscores = weights * (dweights - jnp.sum(dweights * weights, axis=1, keepdims=True))
        dscores = jnp.where(mask, dscores, 0.0) * (1.0 / math.sqrt(HD))
        dscores = dscores.astype(BF16)
        grads.append((dot(dscores, k), dot_tl(dscores, q), dvalue))
    dq, dk, dv = (jnp.concatenate(g, axis=1).astype(BF16) for g in zip(*grads))
    along = jnp.zeros((rows, wide), F32)
    for u in range(parts // 2):
        span = slice(wide * u, wide * (u + 1))
        grown = dot_t(dq, wq_ref[span, :]) + dot_t(dk, wk_ref[span, :]) + dot_t(dv, wv_ref[span, :])
        grown = grown * gain_ref[:, span]
        ds[:, span] = grown
        along = along + grown * xs[:, span].astype(F32)
    factor = jnp.sum(along, axis=1, keepdims=True) * (inverse * inverse * inverse) * (1.0 / width)
    for u in range(parts // 2):
        span = slice(wide * u, wide * (u + 1))
        out = (ds[:, span] * inverse - xs[:, span].astype(F32) * factor).astype(BF16)
        for i in range(2):
            t = 2 * u + i
            cols = slice(share * i, share * (i + 1))
            terms[t % runs, t // runs] = jnp.concatenate([out[:half, cols], out[half:, cols]], axis=1)
    at = lax.axis_index("run")
    stay_ref[...] = terms[at]
    up_ref[...] = terms[lax.rem(at + 1, runs)]
    down_ref[...] = terms[lax.rem(at + runs - 1, runs)]


def kernel_call(body, outs, scratch, args):
    vmem = pl.BlockSpec(memory_space=pltpu.VMEM)
    specs = [pl.BlockSpec(memory_space=pltpu.SMEM)] + [vmem] * (len(args) - 1)
    return pl.pallas_call(
        body,
        out_shape=outs,
        in_specs=specs,
        out_specs=jax.tree.map(lambda _: vmem, outs),
        scratch_shapes=scratch,
        compiler_params=pltpu.CompilerParams(vmem_limit_bytes=VMEM_LIMIT),
    )(*args)


VMEM_LIMIT = 16 * 2**20


def forward_term(offsets, blocks, gain, wq, wk, wv, wo):
    lines, rows, wide = blocks[0].shape
    width = gain.shape[1]
    runs = len(blocks)
    outs = (
        jax.ShapeDtypeStruct((runs * lines, rows // 2, wide), BF16),
        jax.ShapeDtypeStruct((rows, wo.shape[0]), BF16),
    )
    scratch = [
        pltpu.VMEM((runs, lines, rows, wide), BF16),
        pltpu.VMEM((rows, width), BF16),
        pltpu.VMEM((rows, width), BF16),
    ]
    return kernel_call(forward_kernel, outs, scratch, (offsets, *blocks, gain, wq, wk, wv, wo))


def backward_term(offsets, blocks, dctx, gain, wq, wk, wv):
    lines, half, wide = blocks[0].shape
    width = gain.shape[1]
    runs = len(blocks)
    outs = (jax.ShapeDtypeStruct((lines, half, wide), BF16),) * runs
    scratch = [
        pltpu.VMEM((runs, lines, half, wide), BF16),
        pltpu.VMEM((runs, lines, half, wide), BF16),
        pltpu.VMEM((2 * half, width), BF16),
        pltpu.VMEM((2 * half, width), BF16),
        pltpu.VMEM((2 * half, width), F32),
    ]
    return kernel_call(backward_kernel, outs, scratch, (offsets, *blocks, dctx, gain, wq, wk, wv))


def folded(block):
    half = block.shape[0] // 2
    return jnp.concatenate([block[:half], block[half:]], axis=1)


def unfolded(block):
    share = block.shape[1] // 2
    return jnp.concatenate([block[:, :share], block[:, share:]], axis=0)


SECTION = ("x", "far", "core")
TENSOR = ("line", "run")
RUN = 3


def passed_along(block, distance):
    devices = range(lax.axis_size(SECTION))
    route = [(i - distance, i) for i in devices if i - distance in devices]
    return lax.ppermute(block, SECTION, route)


def around(block, axis, distance):
    count = lax.axis_size(axis)
    return lax.ppermute(block, axis, [(i, (i + distance) % count) for i in range(count)])


def mirrored(values, mask):
    section_count = lax.axis_size(SECTION)
    half = section_count // 2

    def swap_by(distance):
        route = [(i, i ^ distance) for i in range(section_count)]
        return lambda held: lax.ppermute(held, SECTION, route)

    return lax.switch(mask - half, [swap_by(half + i) for i in range(half)], values)


def exchanged(blocks, axes):
    return lax.all_to_all(blocks, axes, 0, 0, tiled=True)


def spread(block):
    own = exchanged(jnp.broadcast_to(block[None], (lax.axis_size("line"),) + block.shape), "line")
    return own, around(own, "run", 1), around(own, "run", -1)


def total(rows, blocks):
    summed = jnp.sum(blocks.astype(F32), axis=0)
    return unfolded((folded(rows).astype(F32) + summed).astype(BF16))


def local(fwd_input, bwd_grad, parked, norm_gain, w_query, w_key, w_value, w_out, offsets, mirror):
    fwd_rows = fwd_input[0]
    grad_rows = bwd_grad[0]
    half = fwd_rows.shape[0] // 2
    pair = spread(jnp.concatenate([fwd_rows, grad_rows], axis=1))
    swapped = mirrored(jnp.concatenate([folded(fwd_rows), folded(parked[0])], axis=0), mirror[0])
    back = spread(swapped[half:])
    parked_rows = unfolded(swapped[:half])
    term, dctx = forward_term(offsets, pair, norm_gain, w_query[0], w_key[0], w_value[0], w_out[0])
    layer_out = total(fwd_rows, exchanged(term, TENSOR))
    next_rows = passed_along(layer_out, 1)
    stay, up, down = backward_term(offsets, back, dctx, norm_gain, w_query[0], w_key[0], w_value[0])
    low = around(up, "run", 1)
    high = around(down, "run", -1)
    column = (stay.astype(F32) + low.astype(F32) + high.astype(F32)).astype(BF16)
    grad_out = total(grad_rows, exchanged(column, "line"))
    prev_rows = passed_along(grad_out, -1)
    return (next_rows[None], prev_rows[None], parked_rows[None])


def finer(mesh):
    tensor = mesh.shape["tensor"]
    x = math.isqrt(mesh.shape["section"] // 2)
    shape = (x, mesh.shape["section"] // 2 // x, 2, tensor // RUN, RUN)
    return Mesh(mesh.devices.reshape(shape), SECTION + TENSOR)


def solution(mesh):
    in_specs = (
        P(SECTION, None, TENSOR),
        P(SECTION, None, TENSOR),
        P(SECTION, None, TENSOR),
        P(SECTION, None),
        P(SECTION, None, TENSOR),
        P(SECTION, None, TENSOR),
        P(SECTION, None, TENSOR),
        P(SECTION, TENSOR, None),
        P(SECTION, None, None),
        P(),
    )
    out_specs = (
        P(SECTION, None, TENSOR),
        P(SECTION, None, TENSOR),
        P(SECTION, None, TENSOR),
    )
    return jax.shard_map(local, mesh=finer(mesh), in_specs=in_specs, out_specs=out_specs, check_vma=False)
```

```python
import math

import jax
import jax.numpy as jnp
from jax import lax
from jax.experimental import pallas as pl
from jax.experimental.pallas import tpu as pltpu
from jax.sharding import Mesh
from jax.sharding import PartitionSpec as P

HD = 64
EPS = 1e-05
F32 = jnp.float32
BF16 = jnp.bfloat16


def dot(a, b):
    return jnp.dot(a, b, preferred_element_type=F32)


def dot_t(a, b):
    return lax.dot_general(a, b, (((1,), (1,)), ((), ())), preferred_element_type=F32)


def dot_tl(a, b):
    return lax.dot_general(a, b, (((0,), (0,)), ((), ())), preferred_element_type=F32)


def causal(off_ref, which, rows):
    row = lax.broadcasted_iota(jnp.int32, (rows, rows), 0)
    col = lax.broadcasted_iota(jnp.int32, (rows, rows), 1)
    row_start = jnp.zeros((rows, rows), jnp.int32)
    col_start = jnp.zeros((rows, rows), jnp.int32)
    for c in range(off_ref.shape[2]):
        start = off_ref[0, which, c]
        row_start = jnp.where((row >> 3) == c, start, row_start)
        col_start = jnp.where((col >> 3) == c, start, col_start)
    return row_start + (row & 7) >= col_start + (col & 7)


def softmax(queries, keys, mask):
    scores = dot_t(queries, keys) * (1.0 / math.sqrt(HD))
    scores = jnp.where(mask, scores, -1e30)
    top = jnp.max(scores, axis=1, keepdims=True)
    grown = jnp.exp(scores - top)
    return grown / jnp.sum(grown, axis=1, keepdims=True)


def heads_of(*arrays):
    count = arrays[0].shape[1] // HD
    return [tuple(a[:, h * HD : (h + 1) * HD] for a in arrays) for h in range(count)]


def gathered(own_ref, low_ref, high_ref, all_ref):
    count = all_ref.shape[0]
    at = lax.axis_index("run")
    all_ref[at] = own_ref[...]
    all_ref[lax.rem(at + count - 1, count)] = low_ref[...]
    all_ref[lax.rem(at + 1, count)] = high_ref[...]


def fetches(sources, targets, sems):
    copies = []
    for n, (source, target) in enumerate(zip(sources, targets)):
        step = source.shape[0] // PIECES
        pieces = [
            pltpu.make_async_copy(source.at[pl.ds(i * step, step)], target.at[pl.ds(i * step, step)], sems.at[n, i])
            for i in range(PIECES)
        ]
        for piece in pieces:
            piece.start()
        copies.append(pieces)
    return copies


def arrive(pieces):
    for piece in pieces:
        piece.wait()


def forward_kernel(
    off_ref,
    own_ref,
    low_ref,
    high_ref,
    gain_ref,
    wq_hbm,
    wk_hbm,
    wv_hbm,
    wo_hbm,
    term_ref,
    dctx_ref,
    blocks,
    xs,
    gs,
    wq_ref,
    wk_ref,
    wv_ref,
    wo_ref,
    sems,
):
    wq_in, wk_in, wv_in, wo_in = fetches(
        (wq_hbm, wk_hbm, wv_hbm, wo_hbm), (wq_ref, wk_ref, wv_ref, wo_ref), sems
    )
    gathered(own_ref, low_ref, high_ref, blocks)
    runs, lines, rows, wide = blocks.shape
    parts = runs * lines
    share = wide // 2
    half = rows // 2
    width = parts * share
    squares = jnp.zeros((rows, wide), F32)
    for u in range(parts // 2):
        a = blocks[(2 * u) % runs, (2 * u) // runs]
        b = blocks[(2 * u + 1) % runs, (2 * u + 1) // runs]
        span = slice(wide * u, wide * (u + 1))
        x = jnp.concatenate([a[:, :share], b[:, :share]], axis=1)
        xs[:, span] = x
        gs[:, span] = jnp.concatenate([a[:, share:], b[:, share:]], axis=1)
        x = x.astype(F32)
        squares = squares + x * x
    inverse = lax.rsqrt(jnp.sum(squares, axis=1, keepdims=True) * (1.0 / width) + EPS)
    for u in range(parts // 2):
        span = slice(wide * u, wide * (u + 1))
        xs[:, span] = (xs[:, span].astype(F32) * inverse * gain_ref[:, span]).astype(BF16)
    normed = xs[...]
    arrive(wq_in)
    queries = dot(normed, wq_ref[...]).astype(BF16)
    arrive(wk_in)
    keys = dot(normed, wk_ref[...]).astype(BF16)
    arrive(wv_in)
    values = dot(normed, wv_ref[...]).astype(BF16)
    mask = causal(off_ref, 0, rows)
    context = jnp.concatenate(
        [dot(softmax(q, k, mask).astype(BF16), v) for q, k, v in heads_of(queries, keys, values)], axis=1
    ).astype(BF16)
    arrive(wo_in)
    for u in range(parts // 2):
        span = slice(wide * u, wide * (u + 1))
        out = dot(context, wo_ref[:, span]).astype(BF16)
        term_ref[2 * u] = jnp.concatenate([out[:half, :share], out[half:, :share]], axis=1)
        term_ref[2 * u + 1] = jnp.concatenate([out[:half, share:], out[half:, share:]], axis=1)
    dctx_ref[...] = dot_t(gs[...], wo_ref[...]).astype(BF16)


def backward_kernel(
    off_ref,
    own_ref,
    low_ref,
    high_ref,
    dctx_ref,
    gain_ref,
    wq_hbm,
    wk_hbm,
    wv_hbm,
    stay_ref,
    up_ref,
    down_ref,
    blocks,
    terms,
    xs,
    ns,
    ds,
    wq_ref,
    wk_ref,
    wv_ref,
    sems,
):
    wq_in, wk_in, wv_in = fetches((wq_hbm, wk_hbm, wv_hbm), (wq_ref, wk_ref, wv_ref), sems)
    gathered(own_ref, low_ref, high_ref, blocks)
    runs, lines, half, wide = blocks.shape
    parts = runs * lines
    share = wide // 2
    rows = half * 2
    width = parts * share
    squares = jnp.zeros((rows, wide), F32)
    for u in range(parts // 2):
        a = blocks[(2 * u) % runs, (2 * u) // runs]
        b = blocks[(2 * u + 1) % runs, (2 * u + 1) // runs]
        span = slice(wide * u, wide * (u + 1))
        x = jnp.concatenate(
            [
                jnp.concatenate([a[:, :share], b[:, :share]], axis=1),
                jnp.concatenate([a[:, share:], b[:, share:]], axis=1),
            ],
            axis=0,
        )
        xs[:, span] = x
        x = x.astype(F32)
        squares = squares + x * x
    inverse = lax.rsqrt(jnp.sum(squares, axis=1, keepdims=True) * (1.0 / width) + EPS)
    for u in range(parts // 2):
        span = slice(wide * u, wide * (u + 1))
        ns[:, span] = (xs[:, span].astype(F32) * inverse * gain_ref[:, span]).astype(BF16)
    normed = ns[...]
    arrive(wq_in)
    queries = dot(normed, wq_ref[...]).astype(BF16)
    arrive(wk_in)
    keys = dot(normed, wk_ref[...]).astype(BF16)
    arrive(wv_in)
    values = dot(normed, wv_ref[...]).astype(BF16)
    mask = causal(off_ref, 1, rows)
    grads = []
    for q, k, v, dc in heads_of(queries, keys, values, dctx_ref[...]):
        weights = softmax(q, k, mask)
        dvalue = dot_tl(weights.astype(BF16), dc)
        dweights = dot_t(dc, v).astype(BF16).astype(F32)
        dscores = weights * (dweights - jnp.sum(dweights * weights, axis=1, keepdims=True))
        dscores = jnp.where(mask, dscores, 0.0) * (1.0 / math.sqrt(HD))
        dscores = dscores.astype(BF16)
        grads.append((dot(dscores, k), dot_tl(dscores, q), dvalue))
    dq, dk, dv = (jnp.concatenate(g, axis=1).astype(BF16) for g in zip(*grads))
    along = jnp.zeros((rows, wide), F32)
    for u in range(parts // 2):
        span = slice(wide * u, wide * (u + 1))
        grown = dot_t(dq, wq_ref[span, :]) + dot_t(dk, wk_ref[span, :]) + dot_t(dv, wv_ref[span, :])
        grown = grown * gain_ref[:, span]
        ds[:, span] = grown
        along = along + grown * xs[:, span].astype(F32)
    factor = jnp.sum(along, axis=1, keepdims=True) * (inverse * inverse * inverse) * (1.0 / width)
    for u in range(parts // 2):
        span = slice(wide * u, wide * (u + 1))
        out = (ds[:, span] * inverse - xs[:, span].astype(F32) * factor).astype(BF16)
        for i in range(2):
            t = 2 * u + i
            cols = slice(share * i, share * (i + 1))
            terms[t % runs, t // runs] = jnp.concatenate([out[:half, cols], out[half:, cols]], axis=1)
    at = lax.axis_index("run")
    stay_ref[...] = terms[at]
    up_ref[...] = terms[lax.rem(at + 1, runs)]
    down_ref[...] = terms[lax.rem(at + runs - 1, runs)]


def kernel_call(body, outs, scratch, offsets, args, weights):
    vmem = pl.BlockSpec(memory_space=pltpu.VMEM)
    specs = [pl.BlockSpec(memory_space=pltpu.SMEM)] + [vmem] * len(args)
    specs += [pl.BlockSpec(memory_space=pltpu.HBM)] * len(weights)
    scratch = scratch + [pltpu.VMEM(w.shape, w.dtype) for w in weights]
    scratch.append(pltpu.SemaphoreType.DMA((len(weights), PIECES)))
    return pl.pallas_call(
        body,
        out_shape=outs,
        in_specs=specs,
        out_specs=jax.tree.map(lambda _: vmem, outs),
        scratch_shapes=scratch,
        compiler_params=pltpu.CompilerParams(vmem_limit_bytes=VMEM_LIMIT),
    )(offsets, *args, *[pltpu.with_memory_space_constraint(w, pltpu.HBM) for w in weights])


PIECES = 2
VMEM_LIMIT = 16 * 2**20


def forward_term(offsets, blocks, gain, wq, wk, wv, wo):
    lines, rows, wide = blocks[0].shape
    width = gain.shape[1]
    runs = len(blocks)
    outs = (
        jax.ShapeDtypeStruct((runs * lines, rows // 2, wide), BF16),
        jax.ShapeDtypeStruct((rows, wo.shape[0]), BF16),
    )
    scratch = [
        pltpu.VMEM((runs, lines, rows, wide), BF16),
        pltpu.VMEM((rows, width), BF16),
        pltpu.VMEM((rows, width), BF16),
    ]
    return kernel_call(forward_kernel, outs, scratch, offsets, (*blocks, gain), (wq, wk, wv, wo))


def backward_term(offsets, blocks, dctx, gain, wq, wk, wv):
    lines, half, wide = blocks[0].shape
    width = gain.shape[1]
    runs = len(blocks)
    outs = (jax.ShapeDtypeStruct((lines, half, wide), BF16),) * runs
    scratch = [
        pltpu.VMEM((runs, lines, half, wide), BF16),
        pltpu.VMEM((runs, lines, half, wide), BF16),
        pltpu.VMEM((2 * half, width), BF16),
        pltpu.VMEM((2 * half, width), BF16),
        pltpu.VMEM((2 * half, width), F32),
    ]
    return kernel_call(backward_kernel, outs, scratch, offsets, (*blocks, dctx, gain), (wq, wk, wv))


def folded(block):
    half = block.shape[0] // 2
    return jnp.concatenate([block[:half], block[half:]], axis=1)


def unfolded(block):
    share = block.shape[1] // 2
    return jnp.concatenate([block[:, :share], block[:, share:]], axis=0)


SECTION = ("x", "far", "core")
TENSOR = ("line", "run")
RUN = 3


def passed_along(block, distance):
    devices = range(lax.axis_size(SECTION))
    route = [(i - distance, i) for i in devices if i - distance in devices]
    return lax.ppermute(block, SECTION, route)


def around(block, axis, distance):
    count = lax.axis_size(axis)
    return lax.ppermute(block, axis, [(i, (i + distance) % count) for i in range(count)])


def mirrored(values, mask):
    section_count = lax.axis_size(SECTION)
    half = section_count // 2

    def swap_by(distance):
        route = [(i, i ^ distance) for i in range(section_count)]
        return lambda held: lax.ppermute(held, SECTION, route)

    return lax.switch(mask - half, [swap_by(half + i) for i in range(half)], values)


def exchanged(blocks, axes):
    return lax.all_to_all(blocks, axes, 0, 0, tiled=True)


def spread(block):
    own = exchanged(jnp.broadcast_to(block[None], (lax.axis_size("line"),) + block.shape), "line")
    return own, around(own, "run", 1), around(own, "run", -1)


def total(rows, blocks):
    summed = jnp.sum(blocks.astype(F32), axis=0)
    return unfolded((folded(rows).astype(F32) + summed).astype(BF16))


def local(fwd_input, bwd_grad, parked, norm_gain, w_query, w_key, w_value, w_out, offsets, mirror):
    fwd_rows = fwd_input[0]
    grad_rows = bwd_grad[0]
    half = fwd_rows.shape[0] // 2
    pair = spread(jnp.concatenate([fwd_rows, grad_rows], axis=1))
    swapped = mirrored(jnp.concatenate([folded(fwd_rows), folded(parked[0])], axis=0), mirror[0])
    back = spread(swapped[half:])
    parked_rows = unfolded(swapped[:half])
    term, dctx = forward_term(offsets, pair, norm_gain, w_query[0], w_key[0], w_value[0], w_out[0])
    layer_out = total(fwd_rows, exchanged(term, TENSOR))
    next_rows = passed_along(layer_out, 1)
    stay, up, down = backward_term(offsets, back, dctx, norm_gain, w_query[0], w_key[0], w_value[0])
    low = around(up, "run", 1)
    high = around(down, "run", -1)
    column = (stay.astype(F32) + low.astype(F32) + high.astype(F32)).astype(BF16)
    grad_out = total(grad_rows, exchanged(column, "line"))
    prev_rows = passed_along(grad_out, -1)
    return (next_rows[None], prev_rows[None], parked_rows[None])


def finer(mesh):
    tensor = mesh.shape["tensor"]
    x = math.isqrt(mesh.shape["section"] // 2)
    shape = (x, mesh.shape["section"] // 2 // x, 2, tensor // RUN, RUN)
    return Mesh(mesh.devices.reshape(shape), SECTION + TENSOR)


def solution(mesh):
    in_specs = (
        P(SECTION, None, TENSOR),
        P(SECTION, None, TENSOR),
        P(SECTION, None, TENSOR),
        P(SECTION, None),
        P(SECTION, None, TENSOR),
        P(SECTION, None, TENSOR),
        P(SECTION, None, TENSOR),
        P(SECTION, TENSOR, None),
        P(SECTION, None, None),
        P(),
    )
    out_specs = (
        P(SECTION, None, TENSOR),
        P(SECTION, None, TENSOR),
        P(SECTION, None, TENSOR),
    )
    return jax.shard_map(local, mesh=finer(mesh), in_specs=in_specs, out_specs=out_specs, check_vma=False)
```

```python
import math

import jax
import jax.numpy as jnp
from jax import lax
from jax.experimental import pallas as pl
from jax.experimental.pallas import tpu as pltpu
from jax.sharding import Mesh
from jax.sharding import PartitionSpec as P

HD = 64
EPS = 1e-05
F32 = jnp.float32
BF16 = jnp.bfloat16


def dot(a, b):
    return jnp.dot(a, b, preferred_element_type=F32)


def dot_t(a, b):
    return lax.dot_general(a, b, (((1,), (1,)), ((), ())), preferred_element_type=F32)


def dot_tl(a, b):
    return lax.dot_general(a, b, (((0,), (0,)), ((), ())), preferred_element_type=F32)


def causal(off_ref, which, rows):
    row = lax.broadcasted_iota(jnp.int32, (rows, rows), 0)
    col = lax.broadcasted_iota(jnp.int32, (rows, rows), 1)
    row_start = jnp.zeros((rows, rows), jnp.int32)
    col_start = jnp.zeros((rows, rows), jnp.int32)
    for c in range(off_ref.shape[2]):
        start = off_ref[0, which, c]
        row_start = jnp.where((row >> 3) == c, start, row_start)
        col_start = jnp.where((col >> 3) == c, start, col_start)
    return row_start + (row & 7) >= col_start + (col & 7)


def softmax(queries, keys, mask):
    scores = dot_t(queries, keys) * (1.0 / math.sqrt(HD))
    scores = jnp.where(mask, scores, -1e30)
    top = jnp.max(scores, axis=1, keepdims=True)
    grown = jnp.exp(scores - top)
    return grown / jnp.sum(grown, axis=1, keepdims=True)


def heads_of(*arrays):
    count = arrays[0].shape[1] // HD
    return [tuple(a[:, h * HD : (h + 1) * HD] for a in arrays) for h in range(count)]


def gathered(own_ref, low_ref, high_ref, all_ref):
    count = all_ref.shape[0]
    at = lax.axis_index("run")
    all_ref[at] = own_ref[...]
    all_ref[lax.rem(at + count - 1, count)] = low_ref[...]
    all_ref[lax.rem(at + 1, count)] = high_ref[...]


def fetches(sources, targets, sems):
    copies = []
    for n, (source, target) in enumerate(zip(sources, targets)):
        step = source.shape[0] // PIECES
        pieces = [
            pltpu.make_async_copy(source.at[pl.ds(i * step, step)], target.at[pl.ds(i * step, step)], sems.at[n, i])
            for i in range(PIECES)
        ]
        for piece in pieces:
            piece.start()
        copies.append(pieces)
    return copies


def arrive(pieces):
    for piece in pieces:
        piece.wait()


def forward_kernel(
    off_ref,
    own_ref,
    low_ref,
    high_ref,
    gain_ref,
    wq_hbm,
    wk_hbm,
    wv_hbm,
    wo_hbm,
    term_ref,
    dctx_ref,
    blocks,
    xs,
    gs,
    wq_ref,
    wk_ref,
    wv_ref,
    wo_ref,
    sems,
):
    wq_in, wk_in, wv_in, wo_in = fetches(
        (wq_hbm, wk_hbm, wv_hbm, wo_hbm), (wq_ref, wk_ref, wv_ref, wo_ref), sems
    )
    gathered(own_ref, low_ref, high_ref, blocks)
    runs, lines, rows, wide = blocks.shape
    parts = runs * lines
    share = wide // 2
    half = rows // 2
    width = parts * share
    squares = jnp.zeros((rows, wide), F32)
    for u in range(parts // 2):
        a = blocks[(2 * u) % runs, (2 * u) // runs]
        b = blocks[(2 * u + 1) % runs, (2 * u + 1) // runs]
        span = slice(wide * u, wide * (u + 1))
        x = jnp.concatenate([a[:, :share], b[:, :share]], axis=1)
        xs[:, span] = x
        gs[:, span] = jnp.concatenate([a[:, share:], b[:, share:]], axis=1)
        x = x.astype(F32)
        squares = squares + x * x
    inverse = lax.rsqrt(jnp.sum(squares, axis=1, keepdims=True) * (1.0 / width) + EPS)
    for u in range(parts // 2):
        span = slice(wide * u, wide * (u + 1))
        xs[:, span] = (xs[:, span].astype(F32) * inverse * gain_ref[:, span]).astype(BF16)
    normed = xs[...]
    arrive(wq_in)
    queries = dot(normed, wq_ref[...]).astype(BF16)
    arrive(wk_in)
    keys = dot(normed, wk_ref[...]).astype(BF16)
    arrive(wv_in)
    values = dot(normed, wv_ref[...]).astype(BF16)
    mask = causal(off_ref, 0, rows)
    context = jnp.concatenate(
        [dot(softmax(q, k, mask).astype(BF16), v) for q, k, v in heads_of(queries, keys, values)], axis=1
    ).astype(BF16)
    arrive(wo_in)
    for u in range(parts // 2):
        span = slice(wide * u, wide * (u + 1))
        out = dot(context, wo_ref[:, span]).astype(BF16)
        term_ref[2 * u] = jnp.concatenate([out[:half, :share], out[half:, :share]], axis=1)
        term_ref[2 * u + 1] = jnp.concatenate([out[:half, share:], out[half:, share:]], axis=1)
    dctx_ref[...] = dot_t(gs[...], wo_ref[...]).astype(BF16)


def backward_kernel(
    off_ref,
    own_ref,
    low_ref,
    high_ref,
    forward_ref,
    dctx_ref,
    gain_ref,
    wq_hbm,
    wk_hbm,
    wv_hbm,
    term_ref,
    blocks,
    xs,
    ns,
    ds,
    wq_ref,
    wk_ref,
    wv_ref,
    sems,
):
    wq_in, wk_in, wv_in = fetches((wq_hbm, wk_hbm, wv_hbm), (wq_ref, wk_ref, wv_ref), sems)
    term_ref[:, : forward_ref.shape[1], :] = forward_ref[...]
    gathered(own_ref, low_ref, high_ref, blocks)
    runs, lines, half, wide = blocks.shape
    parts = runs * lines
    share = wide // 2
    rows = half * 2
    width = parts * share
    squares = jnp.zeros((rows, wide), F32)
    for u in range(parts // 2):
        a = blocks[(2 * u) % runs, (2 * u) // runs]
        b = blocks[(2 * u + 1) % runs, (2 * u + 1) // runs]
        span = slice(wide * u, wide * (u + 1))
        x = jnp.concatenate(
            [
                jnp.concatenate([a[:, :share], b[:, :share]], axis=1),
                jnp.concatenate([a[:, share:], b[:, share:]], axis=1),
            ],
            axis=0,
        )
        xs[:, span] = x
        x = x.astype(F32)
        squares = squares + x * x
    inverse = lax.rsqrt(jnp.sum(squares, axis=1, keepdims=True) * (1.0 / width) + EPS)
    for u in range(parts // 2):
        span = slice(wide * u, wide * (u + 1))
        ns[:, span] = (xs[:, span].astype(F32) * inverse * gain_ref[:, span]).astype(BF16)
    normed = ns[...]
    arrive(wq_in)
    queries = dot(normed, wq_ref[...]).astype(BF16)
    arrive(wk_in)
    keys = dot(normed, wk_ref[...]).astype(BF16)
    arrive(wv_in)
    values = dot(normed, wv_ref[...]).astype(BF16)
    mask = causal(off_ref, 1, rows)
    grads = []
    for q, k, v, dc in heads_of(queries, keys, values, dctx_ref[...]):
        weights = softmax(q, k, mask)
        dvalue = dot_tl(weights.astype(BF16), dc)
        dweights = dot_t(dc, v).astype(BF16).astype(F32)
        dscores = weights * (dweights - jnp.sum(dweights * weights, axis=1, keepdims=True))
        dscores = jnp.where(mask, dscores, 0.0) * (1.0 / math.sqrt(HD))
        dscores = dscores.astype(BF16)
        grads.append((dot(dscores, k), dot_tl(dscores, q), dvalue))
    dq, dk, dv = (jnp.concatenate(g, axis=1).astype(BF16) for g in zip(*grads))
    along = jnp.zeros((rows, wide), F32)
    for u in range(parts // 2):
        span = slice(wide * u, wide * (u + 1))
        grown = dot_t(dq, wq_ref[span, :]) + dot_t(dk, wk_ref[span, :]) + dot_t(dv, wv_ref[span, :])
        grown = grown * gain_ref[:, span]
        ds[:, span] = grown
        along = along + grown * xs[:, span].astype(F32)
    factor = jnp.sum(along, axis=1, keepdims=True) * (inverse * inverse * inverse) * (1.0 / width)
    for u in range(parts // 2):
        span = slice(wide * u, wide * (u + 1))
        out = (ds[:, span] * inverse - xs[:, span].astype(F32) * factor).astype(BF16)
        term_ref[2 * u, half:, :] = jnp.concatenate([out[:half, :share], out[half:, :share]], axis=1)
        term_ref[2 * u + 1, half:, :] = jnp.concatenate([out[:half, share:], out[half:, share:]], axis=1)


def kernel_call(body, outs, scratch, offsets, args, weights):
    vmem = pl.BlockSpec(memory_space=pltpu.VMEM)
    specs = [pl.BlockSpec(memory_space=pltpu.SMEM)] + [vmem] * len(args)
    specs += [pl.BlockSpec(memory_space=pltpu.HBM)] * len(weights)
    scratch = scratch + [pltpu.VMEM(w.shape, w.dtype) for w in weights]
    scratch.append(pltpu.SemaphoreType.DMA((len(weights), PIECES)))
    return pl.pallas_call(
        body,
        out_shape=outs,
        in_specs=specs,
        out_specs=jax.tree.map(lambda _: vmem, outs),
        scratch_shapes=scratch,
        compiler_params=pltpu.CompilerParams(vmem_limit_bytes=VMEM_LIMIT),
    )(offsets, *args, *[pltpu.with_memory_space_constraint(w, pltpu.HBM) for w in weights])


PIECES = 2
VMEM_LIMIT = 16 * 2**20


def forward_term(offsets, blocks, gain, wq, wk, wv, wo):
    lines, rows, wide = blocks[0].shape
    width = gain.shape[1]
    runs = len(blocks)
    outs = (
        jax.ShapeDtypeStruct((runs * lines, rows // 2, wide), BF16),
        jax.ShapeDtypeStruct((rows, wo.shape[0]), BF16),
    )
    scratch = [
        pltpu.VMEM((runs, lines, rows, wide), BF16),
        pltpu.VMEM((rows, width), BF16),
        pltpu.VMEM((rows, width), BF16),
    ]
    return kernel_call(forward_kernel, outs, scratch, offsets, (*blocks, gain), (wq, wk, wv, wo))


def both_terms(offsets, blocks, term, dctx, gain, wq, wk, wv):
    lines, half, wide = blocks[0].shape
    width = gain.shape[1]
    runs = len(blocks)
    outs = jax.ShapeDtypeStruct((runs * lines, 2 * half, wide), BF16)
    scratch = [
        pltpu.VMEM((runs, lines, half, wide), BF16),
        pltpu.VMEM((2 * half, width), BF16),
        pltpu.VMEM((2 * half, width), BF16),
        pltpu.VMEM((2 * half, width), F32),
    ]
    return kernel_call(backward_kernel, outs, scratch, offsets, (*blocks, term, dctx, gain), (wq, wk, wv))


def folded(block):
    half = block.shape[0] // 2
    return jnp.concatenate([block[:half], block[half:]], axis=1)


def unfolded(block):
    share = block.shape[1] // 2
    return jnp.concatenate([block[:, :share], block[:, share:]], axis=0)


SECTION = ("x", "far", "core")
TENSOR = ("line", "run")
RUN = 3


def passed_along(block, distance):
    devices = range(lax.axis_size(SECTION))
    route = [(i - distance, i) for i in devices if i - distance in devices]
    return lax.ppermute(block, SECTION, route)


def around(block, axis, distance):
    count = lax.axis_size(axis)
    return lax.ppermute(block, axis, [(i, (i + distance) % count) for i in range(count)])


def mirrored(values, mask):
    section_count = lax.axis_size(SECTION)
    half = section_count // 2

    def swap_by(distance):
        route = [(i, i ^ distance) for i in range(section_count)]
        return lambda held: lax.ppermute(held, SECTION, route)

    return lax.switch(mask - half, [swap_by(half + i) for i in range(half)], values)


def exchanged(blocks, axes):
    return lax.all_to_all(blocks, axes, 0, 0, tiled=True)


def spread(block):
    own = exchanged(jnp.broadcast_to(block[None], (lax.axis_size("line"),) + block.shape), "line")
    return own, around(own, "run", 1), around(own, "run", -1)


def local(fwd_input, bwd_grad, parked, norm_gain, w_query, w_key, w_value, w_out, offsets, mirror):
    fwd_rows = fwd_input[0]
    grad_rows = bwd_grad[0]
    half = fwd_rows.shape[0] // 2
    pair = spread(jnp.concatenate([fwd_rows, grad_rows], axis=1))
    swapped = mirrored(jnp.concatenate([folded(fwd_rows), folded(parked[0])], axis=0), mirror[0])
    back = spread(swapped[half:])
    parked_rows = unfolded(swapped[:half])
    term, dctx = forward_term(offsets, pair, norm_gain, w_query[0], w_key[0], w_value[0], w_out[0])
    terms = both_terms(offsets, back, term, dctx, norm_gain, w_query[0], w_key[0], w_value[0])
    summed = jnp.sum(exchanged(terms, TENSOR).astype(F32), axis=0)
    layer_out = unfolded((folded(fwd_rows).astype(F32) + summed[:half]).astype(BF16))
    grad_out = unfolded((folded(grad_rows).astype(F32) + summed[half:]).astype(BF16))
    next_rows = passed_along(layer_out, 1)
    prev_rows = passed_along(grad_out, -1)
    return (next_rows[None], prev_rows[None], parked_rows[None])


def finer(mesh):
    tensor = mesh.shape["tensor"]
    x = math.isqrt(mesh.shape["section"] // 2)
    shape = (x, mesh.shape["section"] // 2 // x, 2, tensor // RUN, RUN)
    return Mesh(mesh.devices.reshape(shape), SECTION + TENSOR)


def solution(mesh):
    in_specs = (
        P(SECTION, None, TENSOR),
        P(SECTION, None, TENSOR),
        P(SECTION, None, TENSOR),
        P(SECTION, None),
        P(SECTION, None, TENSOR),
        P(SECTION, None, TENSOR),
        P(SECTION, None, TENSOR),
        P(SECTION, TENSOR, None),
        P(SECTION, None, None),
        P(),
    )
    out_specs = (
        P(SECTION, None, TENSOR),
        P(SECTION, None, TENSOR),
        P(SECTION, None, TENSOR),
    )
    return jax.shard_map(local, mesh=finer(mesh), in_specs=in_specs, out_specs=out_specs, check_vma=False)
```

```python
import math

import jax
import jax.numpy as jnp
from jax import lax
from jax.experimental import pallas as pl
from jax.experimental.pallas import tpu as pltpu
from jax.sharding import Mesh
from jax.sharding import PartitionSpec as P

HD = 64
EPS = 1e-05
F32 = jnp.float32
BF16 = jnp.bfloat16


def dot(a, b):
    return jnp.dot(a, b, preferred_element_type=F32)


def dot_t(a, b):
    return lax.dot_general(a, b, (((1,), (1,)), ((), ())), preferred_element_type=F32)


def dot_tl(a, b):
    return lax.dot_general(a, b, (((0,), (0,)), ((), ())), preferred_element_type=F32)


def causal(off_ref, which, rows):
    row = lax.broadcasted_iota(jnp.int32, (rows, rows), 0)
    col = lax.broadcasted_iota(jnp.int32, (rows, rows), 1)
    row_start = jnp.zeros((rows, rows), jnp.int32)
    col_start = jnp.zeros((rows, rows), jnp.int32)
    for c in range(off_ref.shape[2]):
        start = off_ref[0, which, c]
        row_start = jnp.where((row >> 3) == c, start, row_start)
        col_start = jnp.where((col >> 3) == c, start, col_start)
    return row_start + (row & 7) >= col_start + (col & 7)


def softmax(queries, keys, mask):
    scores = dot_t(queries, keys) * (1.0 / math.sqrt(HD))
    scores = jnp.where(mask, scores, -1e30)
    top = jnp.max(scores, axis=1, keepdims=True)
    grown = jnp.exp(scores - top)
    return grown / jnp.sum(grown, axis=1, keepdims=True)


def heads_of(*arrays):
    count = arrays[0].shape[1] // HD
    return [tuple(a[:, h * HD : (h + 1) * HD] for a in arrays) for h in range(count)]


def gathered(own_ref, low_ref, high_ref, all_ref):
    count = all_ref.shape[0]
    at = lax.axis_index("run")
    all_ref[at] = own_ref[...]
    all_ref[lax.rem(at + count - 1, count)] = low_ref[...]
    all_ref[lax.rem(at + 1, count)] = high_ref[...]


def fetches(sources, targets, sems):
    copies = []
    for n, (source, target) in enumerate(zip(sources, targets)):
        step = source.shape[0] // PIECES
        pieces = [
            pltpu.make_async_copy(source.at[pl.ds(i * step, step)], target.at[pl.ds(i * step, step)], sems.at[n, i])
            for i in range(PIECES)
        ]
        for piece in pieces:
            piece.start()
        copies.append(pieces)
    return copies


def arrive(pieces):
    for piece in pieces:
        piece.wait()


def forward_kernel(
    off_ref,
    own_ref,
    low_ref,
    high_ref,
    gain_ref,
    wq_hbm,
    wk_hbm,
    wv_hbm,
    wo_hbm,
    term_ref,
    dctx_ref,
    wq_ref,
    wk_ref,
    wv_ref,
    blocks,
    xs,
    gs,
    wo_ref,
    sems,
):
    wq_in, wk_in, wv_in, wo_in = fetches(
        (wq_hbm, wk_hbm, wv_hbm, wo_hbm), (wq_ref, wk_ref, wv_ref, wo_ref), sems
    )
    gathered(own_ref, low_ref, high_ref, blocks)
    runs, lines, rows, wide = blocks.shape
    parts = runs * lines
    share = wide // 2
    half = rows // 2
    width = parts * share
    squares = jnp.zeros((rows, wide), F32)
    for u in range(parts // 2):
        a = blocks[(2 * u) % runs, (2 * u) // runs]
        b = blocks[(2 * u + 1) % runs, (2 * u + 1) // runs]
        span = slice(wide * u, wide * (u + 1))
        x = jnp.concatenate([a[:, :share], b[:, :share]], axis=1)
        xs[:, span] = x
        gs[:, span] = jnp.concatenate([a[:, share:], b[:, share:]], axis=1)
        x = x.astype(F32)
        squares = squares + x * x
    inverse = lax.rsqrt(jnp.sum(squares, axis=1, keepdims=True) * (1.0 / width) + EPS)
    for u in range(parts // 2):
        span = slice(wide * u, wide * (u + 1))
        xs[:, span] = (xs[:, span].astype(F32) * inverse * gain_ref[:, span]).astype(BF16)
    normed = xs[...]
    arrive(wq_in)
    queries = dot(normed, wq_ref[...]).astype(BF16)
    arrive(wk_in)
    keys = dot(normed, wk_ref[...]).astype(BF16)
    arrive(wv_in)
    values = dot(normed, wv_ref[...]).astype(BF16)
    mask = causal(off_ref, 0, rows)
    context = jnp.concatenate(
        [dot(softmax(q, k, mask).astype(BF16), v) for q, k, v in heads_of(queries, keys, values)], axis=1
    ).astype(BF16)
    arrive(wo_in)
    for u in range(parts // 2):
        span = slice(wide * u, wide * (u + 1))
        out = dot(context, wo_ref[:, span]).astype(BF16)
        term_ref[2 * u] = jnp.concatenate([out[:half, :share], out[half:, :share]], axis=1)
        term_ref[2 * u + 1] = jnp.concatenate([out[:half, share:], out[half:, share:]], axis=1)
    dctx_ref[...] = dot_t(gs[...], wo_ref[...]).astype(BF16)


def backward_kernel(
    off_ref,
    own_ref,
    low_ref,
    high_ref,
    forward_ref,
    dctx_ref,
    gain_ref,
    wq_ref,
    wk_ref,
    wv_ref,
    term_ref,
    blocks,
    xs,
    ns,
    ds,
):
    term_ref[:, : forward_ref.shape[1], :] = forward_ref[...]
    gathered(own_ref, low_ref, high_ref, blocks)
    runs, lines, half, wide = blocks.shape
    parts = runs * lines
    share = wide // 2
    rows = half * 2
    width = parts * share
    squares = jnp.zeros((rows, wide), F32)
    for u in range(parts // 2):
        a = blocks[(2 * u) % runs, (2 * u) // runs]
        b = blocks[(2 * u + 1) % runs, (2 * u + 1) // runs]
        span = slice(wide * u, wide * (u + 1))
        x = jnp.concatenate(
            [
                jnp.concatenate([a[:, :share], b[:, :share]], axis=1),
                jnp.concatenate([a[:, share:], b[:, share:]], axis=1),
            ],
            axis=0,
        )
        xs[:, span] = x
        x = x.astype(F32)
        squares = squares + x * x
    inverse = lax.rsqrt(jnp.sum(squares, axis=1, keepdims=True) * (1.0 / width) + EPS)
    for u in range(parts // 2):
        span = slice(wide * u, wide * (u + 1))
        ns[:, span] = (xs[:, span].astype(F32) * inverse * gain_ref[:, span]).astype(BF16)
    normed = ns[...]
    queries = dot(normed, wq_ref[...]).astype(BF16)
    keys = dot(normed, wk_ref[...]).astype(BF16)
    values = dot(normed, wv_ref[...]).astype(BF16)
    mask = causal(off_ref, 1, rows)
    grads = []
    for q, k, v, dc in heads_of(queries, keys, values, dctx_ref[...]):
        weights = softmax(q, k, mask)
        dvalue = dot_tl(weights.astype(BF16), dc)
        dweights = dot_t(dc, v).astype(BF16).astype(F32)
        dscores = weights * (dweights - jnp.sum(dweights * weights, axis=1, keepdims=True))
        dscores = jnp.where(mask, dscores, 0.0) * (1.0 / math.sqrt(HD))
        dscores = dscores.astype(BF16)
        grads.append((dot(dscores, k), dot_tl(dscores, q), dvalue))
    dq, dk, dv = (jnp.concatenate(g, axis=1).astype(BF16) for g in zip(*grads))
    along = jnp.zeros((rows, wide), F32)
    for u in range(parts // 2):
        span = slice(wide * u, wide * (u + 1))
        grown = dot_t(dq, wq_ref[span, :]) + dot_t(dk, wk_ref[span, :]) + dot_t(dv, wv_ref[span, :])
        grown = grown * gain_ref[:, span]
        ds[:, span] = grown
        along = along + grown * xs[:, span].astype(F32)
    factor = jnp.sum(along, axis=1, keepdims=True) * (inverse * inverse * inverse) * (1.0 / width)
    for u in range(parts // 2):
        span = slice(wide * u, wide * (u + 1))
        out = (ds[:, span] * inverse - xs[:, span].astype(F32) * factor).astype(BF16)
        term_ref[2 * u, half:, :] = jnp.concatenate([out[:half, :share], out[half:, :share]], axis=1)
        term_ref[2 * u + 1, half:, :] = jnp.concatenate([out[:half, share:], out[half:, share:]], axis=1)


def kernel_call(body, outs, scratch, offsets, args, weights=()):
    vmem = pl.BlockSpec(memory_space=pltpu.VMEM)
    specs = [pl.BlockSpec(memory_space=pltpu.SMEM)] + [vmem] * len(args)
    specs += [pl.BlockSpec(memory_space=pltpu.HBM)] * len(weights)
    return pl.pallas_call(
        body,
        out_shape=outs,
        in_specs=specs,
        out_specs=tuple(vmem for _ in outs),
        scratch_shapes=scratch,
        compiler_params=pltpu.CompilerParams(vmem_limit_bytes=VMEM_LIMIT),
    )(offsets, *args, *[pltpu.with_memory_space_constraint(w, pltpu.HBM) for w in weights])


PIECES = 2
VMEM_LIMIT = 16 * 2**20


def forward_term(offsets, blocks, gain, wq, wk, wv, wo):
    lines, rows, wide = blocks[0].shape
    width = gain.shape[1]
    runs = len(blocks)
    outs = (
        jax.ShapeDtypeStruct((runs * lines, rows // 2, wide), BF16),
        jax.ShapeDtypeStruct((rows, wo.shape[0]), BF16),
        *[pltpu.VMEM(w.shape, w.dtype) for w in (wq, wk, wv)],
    )
    scratch = [
        pltpu.VMEM((runs, lines, rows, wide), BF16),
        pltpu.VMEM((rows, width), BF16),
        pltpu.VMEM((rows, width), BF16),
        pltpu.VMEM(wo.shape, wo.dtype),
        pltpu.SemaphoreType.DMA((4, PIECES)),
    ]
    return kernel_call(forward_kernel, outs, scratch, offsets, (*blocks, gain), (wq, wk, wv, wo))


def both_terms(offsets, blocks, term, dctx, gain, wq, wk, wv):
    lines, half, wide = blocks[0].shape
    width = gain.shape[1]
    runs = len(blocks)
    outs = (jax.ShapeDtypeStruct((runs * lines, 2 * half, wide), BF16),)
    scratch = [
        pltpu.VMEM((runs, lines, half, wide), BF16),
        pltpu.VMEM((2 * half, width), BF16),
        pltpu.VMEM((2 * half, width), BF16),
        pltpu.VMEM((2 * half, width), F32),
    ]
    return kernel_call(backward_kernel, outs, scratch, offsets, (*blocks, term, dctx, gain, wq, wk, wv))[0]


def folded(block):
    half = block.shape[0] // 2
    return jnp.concatenate([block[:half], block[half:]], axis=1)


def unfolded(block):
    share = block.shape[1] // 2
    return jnp.concatenate([block[:, :share], block[:, share:]], axis=0)


SECTION = ("x", "far", "core")
TENSOR = ("line", "run")
RUN = 3


def passed_along(block, distance):
    devices = range(lax.axis_size(SECTION))
    route = [(i - distance, i) for i in devices if i - distance in devices]
    return lax.ppermute(block, SECTION, route)


def around(block, axis, distance):
    count = lax.axis_size(axis)
    return lax.ppermute(block, axis, [(i, (i + distance) % count) for i in range(count)])


def mirrored(values, mask):
    section_count = lax.axis_size(SECTION)
    half = section_count // 2

    def swap_by(distance):
        route = [(i, i ^ distance) for i in range(section_count)]
        return lambda held: lax.ppermute(held, SECTION, route)

    return lax.switch(mask - half, [swap_by(half + i) for i in range(half)], values)


def exchanged(blocks, axes):
    return lax.all_to_all(blocks, axes, 0, 0, tiled=True)


def spread(block):
    own = exchanged(jnp.broadcast_to(block[None], (lax.axis_size("line"),) + block.shape), "line")
    return own, around(own, "run", 1), around(own, "run", -1)


def local(fwd_input, bwd_grad, parked, norm_gain, w_query, w_key, w_value, w_out, offsets, mirror):
    fwd_rows = fwd_input[0]
    grad_rows = bwd_grad[0]
    half = fwd_rows.shape[0] // 2
    pair = spread(jnp.concatenate([fwd_rows, grad_rows], axis=1))
    swapped = mirrored(jnp.concatenate([folded(fwd_rows), folded(parked[0])], axis=0), mirror[0])
    back = spread(swapped[half:])
    parked_rows = unfolded(swapped[:half])
    term, dctx, wq, wk, wv = forward_term(offsets, pair, norm_gain, w_query[0], w_key[0], w_value[0], w_out[0])
    terms = both_terms(offsets, back, term, dctx, norm_gain, wq, wk, wv)
    summed = jnp.sum(exchanged(terms, TENSOR).astype(F32), axis=0)
    layer_out = unfolded((folded(fwd_rows).astype(F32) + summed[:half]).astype(BF16))
    grad_out = unfolded((folded(grad_rows).astype(F32) + summed[half:]).astype(BF16))
    next_rows = passed_along(layer_out, 1)
    prev_rows = passed_along(grad_out, -1)
    return (next_rows[None], prev_rows[None], parked_rows[None])


def finer(mesh):
    tensor = mesh.shape["tensor"]
    x = math.isqrt(mesh.shape["section"] // 2)
    shape = (x, mesh.shape["section"] // 2 // x, 2, tensor // RUN, RUN)
    return Mesh(mesh.devices.reshape(shape), SECTION + TENSOR)


def solution(mesh):
    in_specs = (
        P(SECTION, None, TENSOR),
        P(SECTION, None, TENSOR),
        P(SECTION, None, TENSOR),
        P(SECTION, None),
        P(SECTION, None, TENSOR),
        P(SECTION, None, TENSOR),
        P(SECTION, None, TENSOR),
        P(SECTION, TENSOR, None),
        P(SECTION, None, None),
        P(),
    )
    out_specs = (
        P(SECTION, None, TENSOR),
        P(SECTION, None, TENSOR),
        P(SECTION, None, TENSOR),
    )
    return jax.shard_map(local, mesh=finer(mesh), in_specs=in_specs, out_specs=out_specs, check_vma=False)
```

```python
import math

import jax
import jax.numpy as jnp
from jax import lax
from jax.experimental import pallas as pl
from jax.experimental.pallas import tpu as pltpu
from jax.sharding import Mesh
from jax.sharding import PartitionSpec as P

HD = 64
EPS = 1e-05
F32 = jnp.float32
BF16 = jnp.bfloat16


def dot(a, b):
    return jnp.dot(a, b, preferred_element_type=F32)


def dot_t(a, b):
    return lax.dot_general(a, b, (((1,), (1,)), ((), ())), preferred_element_type=F32)


def dot_tl(a, b):
    return lax.dot_general(a, b, (((0,), (0,)), ((), ())), preferred_element_type=F32)


def causal(off_ref, which, rows):
    row = lax.broadcasted_iota(jnp.int32, (rows, rows), 0)
    col = lax.broadcasted_iota(jnp.int32, (rows, rows), 1)
    row_start = jnp.zeros((rows, rows), jnp.int32)
    col_start = jnp.zeros((rows, rows), jnp.int32)
    for c in range(off_ref.shape[2]):
        start = off_ref[0, which, c]
        row_start = jnp.where((row >> 3) == c, start, row_start)
        col_start = jnp.where((col >> 3) == c, start, col_start)
    return row_start + (row & 7) >= col_start + (col & 7)


def softmax(queries, keys, mask):
    scores = dot_t(queries, keys) * (1.0 / math.sqrt(HD))
    scores = jnp.where(mask, scores, -1e30)
    top = jnp.max(scores, axis=1, keepdims=True)
    grown = jnp.exp(scores - top)
    return grown / jnp.sum(grown, axis=1, keepdims=True)


def heads_of(*arrays):
    count = arrays[0].shape[1] // HD
    return [tuple(a[:, h * HD : (h + 1) * HD] for a in arrays) for h in range(count)]


def gathered(own_ref, low_ref, high_ref, all_ref):
    count = all_ref.shape[0]
    at = lax.axis_index("run")
    all_ref[at] = own_ref[...]
    all_ref[lax.rem(at + count - 1, count)] = low_ref[...]
    all_ref[lax.rem(at + 1, count)] = high_ref[...]


def fetches(sources, targets, sems):
    copies = []
    for n, (source, target) in enumerate(zip(sources, targets)):
        step = source.shape[0] // PIECES
        pieces = [
            pltpu.make_async_copy(source.at[pl.ds(i * step, step)], target.at[pl.ds(i * step, step)], sems.at[n, i])
            for i in range(PIECES)
        ]
        for piece in pieces:
            piece.start()
        copies.append(pieces)
    return copies


def arrive(pieces):
    for piece in pieces:
        piece.wait()


def forward_kernel(
    off_ref,
    own_ref,
    low_ref,
    high_ref,
    gain_ref,
    wq_hbm,
    wk_hbm,
    wv_hbm,
    wo_hbm,
    term_ref,
    dctx_ref,
    wq_ref,
    blocks,
    xs,
    gs,
    wk_ref,
    wv_ref,
    wo_ref,
    sems,
):
    wq_in, wk_in, wv_in, wo_in = fetches(
        (wq_hbm, wk_hbm, wv_hbm, wo_hbm), (wq_ref, wk_ref, wv_ref, wo_ref), sems
    )
    gathered(own_ref, low_ref, high_ref, blocks)
    runs, lines, rows, wide = blocks.shape
    parts = runs * lines
    share = wide // 2
    half = rows // 2
    width = parts * share
    squares = jnp.zeros((rows, wide), F32)
    for u in range(parts // 2):
        a = blocks[(2 * u) % runs, (2 * u) // runs]
        b = blocks[(2 * u + 1) % runs, (2 * u + 1) // runs]
        span = slice(wide * u, wide * (u + 1))
        x = jnp.concatenate([a[:, :share], b[:, :share]], axis=1)
        xs[:, span] = x
        gs[:, span] = jnp.concatenate([a[:, share:], b[:, share:]], axis=1)
        x = x.astype(F32)
        squares = squares + x * x
    inverse = lax.rsqrt(jnp.sum(squares, axis=1, keepdims=True) * (1.0 / width) + EPS)
    for u in range(parts // 2):
        span = slice(wide * u, wide * (u + 1))
        xs[:, span] = (xs[:, span].astype(F32) * inverse * gain_ref[:, span]).astype(BF16)
    normed = xs[...]
    arrive(wq_in)
    queries = dot(normed, wq_ref[...]).astype(BF16)
    arrive(wk_in)
    keys = dot(normed, wk_ref[...]).astype(BF16)
    arrive(wv_in)
    values = dot(normed, wv_ref[...]).astype(BF16)
    mask = causal(off_ref, 0, rows)
    context = jnp.concatenate(
        [dot(softmax(q, k, mask).astype(BF16), v) for q, k, v in heads_of(queries, keys, values)], axis=1
    ).astype(BF16)
    arrive(wo_in)
    for u in range(parts // 2):
        span = slice(wide * u, wide * (u + 1))
        out = dot(context, wo_ref[:, span]).astype(BF16)
        term_ref[2 * u] = jnp.concatenate([out[:half, :share], out[half:, :share]], axis=1)
        term_ref[2 * u + 1] = jnp.concatenate([out[:half, share:], out[half:, share:]], axis=1)
    dctx_ref[...] = dot_t(gs[...], wo_ref[...]).astype(BF16)


def backward_kernel(
    off_ref,
    back_ref,
    forward_ref,
    dctx_ref,
    gain_ref,
    wq_ref,
    wk_hbm,
    wv_hbm,
    term_ref,
    xs,
    ns,
    ds,
    wk_ref,
    wv_ref,
    sems,
):
    wk_in, wv_in = fetches((wk_hbm, wv_hbm), (wk_ref, wv_ref), sems)
    term_ref[:, : forward_ref.shape[1], :] = forward_ref[...]
    parts, half, wide = back_ref.shape
    share = wide // 2
    rows = half * 2
    width = parts * share
    squares = jnp.zeros((rows, wide), F32)
    for u in range(parts // 2):
        a = back_ref[2 * u]
        b = back_ref[2 * u + 1]
        span = slice(wide * u, wide * (u + 1))
        x = jnp.concatenate(
            [
                jnp.concatenate([a[:, :share], b[:, :share]], axis=1),
                jnp.concatenate([a[:, share:], b[:, share:]], axis=1),
            ],
            axis=0,
        )
        xs[:, span] = x
        x = x.astype(F32)
        squares = squares + x * x
    inverse = lax.rsqrt(jnp.sum(squares, axis=1, keepdims=True) * (1.0 / width) + EPS)
    for u in range(parts // 2):
        span = slice(wide * u, wide * (u + 1))
        ns[:, span] = (xs[:, span].astype(F32) * inverse * gain_ref[:, span]).astype(BF16)
    normed = ns[...]
    queries = dot(normed, wq_ref[...]).astype(BF16)
    arrive(wk_in)
    keys = dot(normed, wk_ref[...]).astype(BF16)
    arrive(wv_in)
    values = dot(normed, wv_ref[...]).astype(BF16)
    mask = causal(off_ref, 1, rows)
    grads = []
    for q, k, v, dc in heads_of(queries, keys, values, dctx_ref[...]):
        weights = softmax(q, k, mask)
        dvalue = dot_tl(weights.astype(BF16), dc)
        dweights = dot_t(dc, v).astype(BF16).astype(F32)
        dscores = weights * (dweights - jnp.sum(dweights * weights, axis=1, keepdims=True))
        dscores = jnp.where(mask, dscores, 0.0) * (1.0 / math.sqrt(HD))
        dscores = dscores.astype(BF16)
        grads.append((dot(dscores, k), dot_tl(dscores, q), dvalue))
    dq, dk, dv = (jnp.concatenate(g, axis=1).astype(BF16) for g in zip(*grads))
    along = jnp.zeros((rows, wide), F32)
    for u in range(parts // 2):
        span = slice(wide * u, wide * (u + 1))
        grown = dot_t(dq, wq_ref[span, :]) + dot_t(dk, wk_ref[span, :]) + dot_t(dv, wv_ref[span, :])
        grown = grown * gain_ref[:, span]
        ds[:, span] = grown
        along = along + grown * xs[:, span].astype(F32)
    factor = jnp.sum(along, axis=1, keepdims=True) * (inverse * inverse * inverse) * (1.0 / width)
    for u in range(parts // 2):
        span = slice(wide * u, wide * (u + 1))
        out = (ds[:, span] * inverse - xs[:, span].astype(F32) * factor).astype(BF16)
        term_ref[2 * u, half:, :] = jnp.concatenate([out[:half, :share], out[half:, :share]], axis=1)
        term_ref[2 * u + 1, half:, :] = jnp.concatenate([out[:half, share:], out[half:, share:]], axis=1)


def kernel_call(body, outs, scratch, offsets, args, weights=()):
    vmem = pl.BlockSpec(memory_space=pltpu.VMEM)
    specs = [pl.BlockSpec(memory_space=pltpu.SMEM)] + [vmem] * len(args)
    specs += [pl.BlockSpec(memory_space=pltpu.HBM)] * len(weights)
    return pl.pallas_call(
        body,
        out_shape=outs,
        in_specs=specs,
        out_specs=tuple(vmem for _ in outs),
        scratch_shapes=scratch,
        compiler_params=pltpu.CompilerParams(vmem_limit_bytes=VMEM_LIMIT),
    )(offsets, *args, *[pltpu.with_memory_space_constraint(w, pltpu.HBM) for w in weights])


PIECES = 4
VMEM_LIMIT = 16 * 2**20


def forward_term(offsets, blocks, gain, wq, wk, wv, wo):
    lines, rows, wide = blocks[0].shape
    width = gain.shape[1]
    runs = len(blocks)
    outs = (
        jax.ShapeDtypeStruct((runs * lines, rows // 2, wide), BF16),
        jax.ShapeDtypeStruct((rows, wo.shape[0]), BF16),
        pltpu.VMEM(wq.shape, wq.dtype),
    )
    scratch = [
        pltpu.VMEM((runs, lines, rows, wide), BF16),
        pltpu.VMEM((rows, width), BF16),
        pltpu.VMEM((rows, width), BF16),
        *[pltpu.VMEM(w.shape, w.dtype) for w in (wk, wv, wo)],
        pltpu.SemaphoreType.DMA((4, PIECES)),
    ]
    return kernel_call(forward_kernel, outs, scratch, offsets, (*blocks, gain), (wq, wk, wv, wo))


def both_terms(offsets, back, term, dctx, gain, wq, wk, wv):
    parts, half, wide = back.shape
    width = gain.shape[1]
    outs = (jax.ShapeDtypeStruct((parts, 2 * half, wide), BF16),)
    scratch = [
        pltpu.VMEM((2 * half, width), BF16),
        pltpu.VMEM((2 * half, width), BF16),
        pltpu.VMEM((2 * half, width), F32),
        *[pltpu.VMEM(w.shape, w.dtype) for w in (wk, wv)],
        pltpu.SemaphoreType.DMA((2, PIECES)),
    ]
    return kernel_call(backward_kernel, outs, scratch, offsets, (back, term, dctx, gain, wq), (wk, wv))[0]


def folded(block):
    half = block.shape[0] // 2
    return jnp.concatenate([block[:half], block[half:]], axis=1)


def unfolded(block):
    share = block.shape[1] // 2
    return jnp.concatenate([block[:, :share], block[:, share:]], axis=0)


SECTION = ("x", "far", "core")
TENSOR = ("line", "run")
RUN = 3


def passed_along(block, distance):
    devices = range(lax.axis_size(SECTION))
    route = [(i - distance, i) for i in devices if i - distance in devices]
    return lax.ppermute(block, SECTION, route)


def around(block, axis, distance):
    count = lax.axis_size(axis)
    return lax.ppermute(block, axis, [(i, (i + distance) % count) for i in range(count)])


def mirrored(values, mask):
    section_count = lax.axis_size(SECTION)
    half = section_count // 2

    def swap_by(distance):
        route = [(i, i ^ distance) for i in range(section_count)]
        return lambda held: lax.ppermute(held, SECTION, route)

    return lax.switch(mask - half, [swap_by(half + i) for i in range(half)], values)


def exchanged(blocks, axes):
    return lax.all_to_all(blocks, axes, 0, 0, tiled=True)


def spread(block):
    return exchanged(repeated(block, TENSOR), TENSOR)


def spread_in_levels(*parts):
    own = exchanged(repeated(jnp.concatenate(parts, axis=1), "line"), "line")
    return own, around(own, "run", 1), around(own, "run", -1)


def repeated(block, axes):
    return jnp.broadcast_to(block[None], (lax.axis_size(axes),) + block.shape)


def local(fwd_input, bwd_grad, parked, norm_gain, w_query, w_key, w_value, w_out, offsets, mirror):
    fwd_rows = fwd_input[0]
    grad_rows = bwd_grad[0]
    half = fwd_rows.shape[0] // 2
    pair = spread_in_levels(fwd_rows, grad_rows)
    swapped = mirrored(jnp.concatenate([folded(fwd_rows), folded(parked[0])], axis=0), mirror[0])
    back = spread(swapped[half:])
    parked_rows = unfolded(swapped[:half])
    term, dctx, wq = forward_term(offsets, pair, norm_gain, w_query[0], w_key[0], w_value[0], w_out[0])
    terms = both_terms(offsets, back, term, dctx, norm_gain, wq, w_key[0], w_value[0])
    summed = jnp.sum(exchanged(terms, TENSOR).astype(F32), axis=0)
    layer_out = unfolded((folded(fwd_rows).astype(F32) + summed[:half]).astype(BF16))
    grad_out = unfolded((folded(grad_rows).astype(F32) + summed[half:]).astype(BF16))
    next_rows = passed_along(layer_out, 1)
    prev_rows = passed_along(grad_out, -1)
    return (next_rows[None], prev_rows[None], parked_rows[None])


def finer(mesh):
    tensor = mesh.shape["tensor"]
    x = math.isqrt(mesh.shape["section"] // 2)
    shape = (x, mesh.shape["section"] // 2 // x, 2, tensor // RUN, RUN)
    return Mesh(mesh.devices.reshape(shape), SECTION + TENSOR)


def solution(mesh):
    in_specs = (
        P(SECTION, None, TENSOR),
        P(SECTION, None, TENSOR),
        P(SECTION, None, TENSOR),
        P(SECTION, None),
        P(SECTION, None, TENSOR),
        P(SECTION, None, TENSOR),
        P(SECTION, None, TENSOR),
        P(SECTION, TENSOR, None),
        P(SECTION, None, None),
        P(),
    )
    out_specs = (
        P(SECTION, None, TENSOR),
        P(SECTION, None, TENSOR),
        P(SECTION, None, TENSOR),
    )
    return jax.shard_map(local, mesh=finer(mesh), in_specs=in_specs, out_specs=out_specs, check_vma=False)
```

```python
import math

import jax
import jax.numpy as jnp
from jax import lax
from jax.experimental import pallas as pl
from jax.experimental.pallas import tpu as pltpu
from jax.sharding import Mesh
from jax.sharding import PartitionSpec as P

HD = 64
EPS = 1e-05
F32 = jnp.float32
BF16 = jnp.bfloat16


def dot(a, b):
    return jnp.dot(a, b, preferred_element_type=F32)


def dot_t(a, b):
    return lax.dot_general(a, b, (((1,), (1,)), ((), ())), preferred_element_type=F32)


def dot_tl(a, b):
    return lax.dot_general(a, b, (((0,), (0,)), ((), ())), preferred_element_type=F32)


def causal(off_ref, which, rows):
    row = lax.broadcasted_iota(jnp.int32, (rows, rows), 0)
    col = lax.broadcasted_iota(jnp.int32, (rows, rows), 1)
    row_start = jnp.zeros((rows, rows), jnp.int32)
    col_start = jnp.zeros((rows, rows), jnp.int32)
    for c in range(off_ref.shape[2]):
        start = off_ref[0, which, c]
        row_start = jnp.where((row >> 3) == c, start, row_start)
        col_start = jnp.where((col >> 3) == c, start, col_start)
    return row_start + (row & 7) >= col_start + (col & 7)


def softmax(queries, keys, mask):
    scores = dot_t(queries, keys) * (1.0 / math.sqrt(HD))
    scores = jnp.where(mask, scores, -1e30)
    top = jnp.max(scores, axis=1, keepdims=True)
    grown = jnp.exp(scores - top)
    return grown / jnp.sum(grown, axis=1, keepdims=True)


def heads_of(*arrays):
    count = arrays[0].shape[1] // HD
    return [tuple(a[:, h * HD : (h + 1) * HD] for a in arrays) for h in range(count)]


def gathered(own_ref, low_ref, high_ref, all_ref):
    count = all_ref.shape[0]
    at = lax.axis_index("run")
    all_ref[at] = own_ref[...]
    all_ref[lax.rem(at + count - 1, count)] = low_ref[...]
    all_ref[lax.rem(at + 1, count)] = high_ref[...]


def fetches(sources, targets, sems):
    copies = []
    for n, (source, target) in enumerate(zip(sources, targets)):
        step = source.shape[0] // PIECES
        pieces = [
            pltpu.make_async_copy(source.at[pl.ds(i * step, step)], target.at[pl.ds(i * step, step)], sems.at[n, i])
            for i in range(PIECES)
        ]
        for piece in pieces:
            piece.start()
        copies.append(pieces)
    return copies


def arrive(pieces):
    for piece in pieces:
        piece.wait()


def forward_kernel(
    off_ref,
    own_ref,
    low_ref,
    high_ref,
    gain_ref,
    wq_hbm,
    wk_hbm,
    wv_hbm,
    wo_hbm,
    term_ref,
    dctx_ref,
    wq_ref,
    wk_ref,
    wv_ref,
    blocks,
    xs,
    gs,
    wo_ref,
    sems,
):
    wq_in, wk_in, wv_in, wo_in = fetches(
        (wq_hbm, wk_hbm, wv_hbm, wo_hbm), (wq_ref, wk_ref, wv_ref, wo_ref), sems
    )
    gathered(own_ref, low_ref, high_ref, blocks)
    runs, lines, rows, wide = blocks.shape
    parts = runs * lines
    share = wide // 2
    half = rows // 2
    width = parts * share
    squares = jnp.zeros((rows, wide), F32)
    for u in range(parts // 2):
        a = blocks[(2 * u) % runs, (2 * u) // runs]
        b = blocks[(2 * u + 1) % runs, (2 * u + 1) // runs]
        span = slice(wide * u, wide * (u + 1))
        x = jnp.concatenate([a[:, :share], b[:, :share]], axis=1)
        xs[:, span] = x
        gs[:, span] = jnp.concatenate([a[:, share:], b[:, share:]], axis=1)
        x = x.astype(F32)
        squares = squares + x * x
    inverse = lax.rsqrt(jnp.sum(squares, axis=1, keepdims=True) * (1.0 / width) + EPS)
    for u in range(parts // 2):
        span = slice(wide * u, wide * (u + 1))
        xs[:, span] = (xs[:, span].astype(F32) * inverse * gain_ref[:, span]).astype(BF16)
    normed = xs[...]
    arrive(wq_in)
    queries = dot(normed, wq_ref[...]).astype(BF16)
    arrive(wk_in)
    keys = dot(normed, wk_ref[...]).astype(BF16)
    arrive(wv_in)
    values = dot(normed, wv_ref[...]).astype(BF16)
    mask = causal(off_ref, 0, rows)
    context = jnp.concatenate(
        [dot(softmax(q, k, mask).astype(BF16), v) for q, k, v in heads_of(queries, keys, values)], axis=1
    ).astype(BF16)
    arrive(wo_in)
    for u in range(parts // 2):
        span = slice(wide * u, wide * (u + 1))
        out = dot(context, wo_ref[:, span]).astype(BF16)
        term_ref[2 * u] = jnp.concatenate([out[:half, :share], out[half:, :share]], axis=1)
        term_ref[2 * u + 1] = jnp.concatenate([out[:half, share:], out[half:, share:]], axis=1)
    dctx_ref[...] = dot_t(gs[...], wo_ref[...]).astype(BF16)


def backward_kernel(
    off_ref,
    columns_ref,
    forward_ref,
    dctx_ref,
    gain_ref,
    wq_ref,
    wk_ref,
    wv_ref,
    term_ref,
    blocks,
    xs,
    ns,
    ds,
):
    term_ref[:, : forward_ref.shape[1], :] = forward_ref[...]
    runs, lines, half, wide = blocks.shape
    gathered(*[columns_ref.at[:, pl.ds(half * i, half), :] for i in range(runs)], blocks)
    parts = runs * lines
    share = wide // 2
    rows = half * 2
    width = parts * share
    squares = jnp.zeros((rows, wide), F32)
    for u in range(parts // 2):
        a = blocks[(2 * u) % runs, (2 * u) // runs]
        b = blocks[(2 * u + 1) % runs, (2 * u + 1) // runs]
        span = slice(wide * u, wide * (u + 1))
        x = jnp.concatenate(
            [
                jnp.concatenate([a[:, :share], b[:, :share]], axis=1),
                jnp.concatenate([a[:, share:], b[:, share:]], axis=1),
            ],
            axis=0,
        )
        xs[:, span] = x
        x = x.astype(F32)
        squares = squares + x * x
    inverse = lax.rsqrt(jnp.sum(squares, axis=1, keepdims=True) * (1.0 / width) + EPS)
    for u in range(parts // 2):
        span = slice(wide * u, wide * (u + 1))
        ns[:, span] = (xs[:, span].astype(F32) * inverse * gain_ref[:, span]).astype(BF16)
    normed = ns[...]
    queries = dot(normed, wq_ref[...]).astype(BF16)
    keys = dot(normed, wk_ref[...]).astype(BF16)
    values = dot(normed, wv_ref[...]).astype(BF16)
    mask = causal(off_ref, 1, rows)
    grads = []
    for q, k, v, dc in heads_of(queries, keys, values, dctx_ref[...]):
        weights = softmax(q, k, mask)
        dvalue = dot_tl(weights.astype(BF16), dc)
        dweights = dot_t(dc, v).astype(BF16).astype(F32)
        dscores = weights * (dweights - jnp.sum(dweights * weights, axis=1, keepdims=True))
        dscores = jnp.where(mask, dscores, 0.0) * (1.0 / math.sqrt(HD))
        dscores = dscores.astype(BF16)
        grads.append((dot(dscores, k), dot_tl(dscores, q), dvalue))
    dq, dk, dv = (jnp.concatenate(g, axis=1).astype(BF16) for g in zip(*grads))
    along = jnp.zeros((rows, wide), F32)
    for u in range(parts // 2):
        span = slice(wide * u, wide * (u + 1))
        grown = dot_t(dq, wq_ref[span, :]) + dot_t(dk, wk_ref[span, :]) + dot_t(dv, wv_ref[span, :])
        grown = grown * gain_ref[:, span]
        ds[:, span] = grown
        along = along + grown * xs[:, span].astype(F32)
    factor = jnp.sum(along, axis=1, keepdims=True) * (inverse * inverse * inverse) * (1.0 / width)
    for u in range(parts // 2):
        span = slice(wide * u, wide * (u + 1))
        out = (ds[:, span] * inverse - xs[:, span].astype(F32) * factor).astype(BF16)
        term_ref[2 * u, half:, :] = jnp.concatenate([out[:half, :share], out[half:, :share]], axis=1)
        term_ref[2 * u + 1, half:, :] = jnp.concatenate([out[:half, share:], out[half:, share:]], axis=1)


def kernel_call(body, outs, scratch, offsets, args, weights=()):
    vmem = pl.BlockSpec(memory_space=pltpu.VMEM)
    specs = [pl.BlockSpec(memory_space=pltpu.SMEM)] + [vmem] * len(args)
    specs += [pl.BlockSpec(memory_space=pltpu.HBM)] * len(weights)
    return pl.pallas_call(
        body,
        out_shape=outs,
        in_specs=specs,
        out_specs=tuple(vmem for _ in outs),
        scratch_shapes=scratch,
        compiler_params=pltpu.CompilerParams(vmem_limit_bytes=VMEM_LIMIT),
    )(offsets, *args, *[pltpu.with_memory_space_constraint(w, pltpu.HBM) for w in weights])


PIECES = 2
VMEM_LIMIT = 16 * 2**20


def forward_term(offsets, blocks, gain, wq, wk, wv, wo):
    lines, rows, wide = blocks[0].shape
    width = gain.shape[1]
    runs = len(blocks)
    outs = (
        jax.ShapeDtypeStruct((runs * lines, rows // 2, wide), BF16),
        jax.ShapeDtypeStruct((rows, wo.shape[0]), BF16),
        *[pltpu.VMEM(w.shape, w.dtype) for w in (wq, wk, wv)],
    )
    scratch = [
        pltpu.VMEM((runs, lines, rows, wide), BF16),
        pltpu.VMEM((rows, width), BF16),
        pltpu.VMEM((rows, width), BF16),
        pltpu.VMEM(wo.shape, wo.dtype),
        pltpu.SemaphoreType.DMA((4, PIECES)),
    ]
    return kernel_call(forward_kernel, outs, scratch, offsets, (*blocks, gain), (wq, wk, wv, wo))


def both_terms(offsets, columns, term, dctx, gain, wq, wk, wv):
    lines, rows, wide = columns.shape
    half = rows // RUN
    runs = RUN
    width = gain.shape[1]
    outs = (jax.ShapeDtypeStruct((runs * lines, 2 * half, wide), BF16),)
    scratch = [
        pltpu.VMEM((runs, lines, half, wide), BF16),
        pltpu.VMEM((2 * half, width), BF16),
        pltpu.VMEM((2 * half, width), BF16),
        pltpu.VMEM((2 * half, width), F32),
    ]
    return kernel_call(backward_kernel, outs, scratch, offsets, (columns, term, dctx, gain, wq, wk, wv))[0]


def folded(block):
    half = block.shape[0] // 2
    return jnp.concatenate([block[:half], block[half:]], axis=1)


def unfolded(block):
    share = block.shape[1] // 2
    return jnp.concatenate([block[:, :share], block[:, share:]], axis=0)


SECTION = ("x", "far", "core")
TENSOR = ("line", "run")
RUN = 3


def passed_along(block, distance):
    devices = range(lax.axis_size(SECTION))
    route = [(i - distance, i) for i in devices if i - distance in devices]
    return lax.ppermute(block, SECTION, route)


def around(block, axis, distance):
    count = lax.axis_size(axis)
    return lax.ppermute(block, axis, [(i, (i + distance) % count) for i in range(count)])


def mirrored(values, mask):
    section_count = lax.axis_size(SECTION)
    half = section_count // 2

    def swap_by(distance):
        route = [(i, i ^ distance) for i in range(section_count)]
        return lambda held: lax.ppermute(held, SECTION, route)

    return lax.switch(mask - half, [swap_by(half + i) for i in range(half)], values)


def exchanged(blocks, axes):
    return lax.all_to_all(blocks, axes, 0, 0, tiled=True)


def spread(block):
    own = exchanged(repeated(block), "line")
    return own, around(own, "run", 1), around(own, "run", -1)


def spread_columns(block):
    column = jnp.concatenate([block, around(block, "run", 1), around(block, "run", -1)], axis=0)
    return exchanged(repeated(column), "line")


def repeated(block):
    return jnp.broadcast_to(block[None], (lax.axis_size("line"),) + block.shape)


def local(fwd_input, bwd_grad, parked, norm_gain, w_query, w_key, w_value, w_out, offsets, mirror):
    fwd_rows = fwd_input[0]
    grad_rows = bwd_grad[0]
    half = fwd_rows.shape[0] // 2
    pair = spread(jnp.concatenate([fwd_rows, grad_rows], axis=1))
    swapped = mirrored(jnp.concatenate([folded(fwd_rows), folded(parked[0])], axis=0), mirror[0])
    back = spread_columns(swapped[half:])
    parked_rows = unfolded(swapped[:half])
    term, dctx, wq, wk, wv = forward_term(offsets, pair, norm_gain, w_query[0], w_key[0], w_value[0], w_out[0])
    terms = both_terms(offsets, back, term, dctx, norm_gain, wq, wk, wv)
    summed = jnp.sum(exchanged(terms, TENSOR).astype(F32), axis=0)
    layer_out = unfolded((folded(fwd_rows).astype(F32) + summed[:half]).astype(BF16))
    grad_out = unfolded((folded(grad_rows).astype(F32) + summed[half:]).astype(BF16))
    next_rows = passed_along(layer_out, 1)
    prev_rows = passed_along(grad_out, -1)
    return (next_rows[None], prev_rows[None], parked_rows[None])


def finer(mesh):
    tensor = mesh.shape["tensor"]
    x = math.isqrt(mesh.shape["section"] // 2)
    shape = (x, mesh.shape["section"] // 2 // x, 2, tensor // RUN, RUN)
    return Mesh(mesh.devices.reshape(shape), SECTION + TENSOR)


def solution(mesh):
    in_specs = (
        P(SECTION, None, TENSOR),
        P(SECTION, None, TENSOR),
        P(SECTION, None, TENSOR),
        P(SECTION, None),
        P(SECTION, None, TENSOR),
        P(SECTION, None, TENSOR),
        P(SECTION, None, TENSOR),
        P(SECTION, TENSOR, None),
        P(SECTION, None, None),
        P(),
    )
    out_specs = (
        P(SECTION, None, TENSOR),
        P(SECTION, None, TENSOR),
        P(SECTION, None, TENSOR),
    )
    return jax.shard_map(local, mesh=finer(mesh), in_specs=in_specs, out_specs=out_specs, check_vma=False)
```

```python
import math

import jax
import jax.numpy as jnp
from jax import lax
from jax.experimental import pallas as pl
from jax.experimental.pallas import tpu as pltpu
from jax.sharding import Mesh
from jax.sharding import PartitionSpec as P

HD = 64
EPS = 1e-05
F32 = jnp.float32
BF16 = jnp.bfloat16


def dot(a, b):
    return jnp.dot(a, b, preferred_element_type=F32)


def dot_t(a, b):
    return lax.dot_general(a, b, (((1,), (1,)), ((), ())), preferred_element_type=F32)


def dot_tl(a, b):
    return lax.dot_general(a, b, (((0,), (0,)), ((), ())), preferred_element_type=F32)


def causal(off_ref, which, rows):
    row = lax.broadcasted_iota(jnp.int32, (rows, rows), 0)
    col = lax.broadcasted_iota(jnp.int32, (rows, rows), 1)
    row_start = jnp.zeros((rows, rows), jnp.int32)
    col_start = jnp.zeros((rows, rows), jnp.int32)
    for c in range(off_ref.shape[2]):
        start = off_ref[0, which, c]
        row_start = jnp.where((row >> 3) == c, start, row_start)
        col_start = jnp.where((col >> 3) == c, start, col_start)
    return row_start + (row & 7) >= col_start + (col & 7)


def softmax(queries, keys, mask):
    scores = dot_t(queries, keys) * (1.0 / math.sqrt(HD))
    scores = jnp.where(mask, scores, -1e30)
    top = jnp.max(scores, axis=1, keepdims=True)
    grown = jnp.exp(scores - top)
    return grown / jnp.sum(grown, axis=1, keepdims=True)


def heads_of(*arrays):
    count = arrays[0].shape[1] // HD
    return [tuple(a[:, h * HD : (h + 1) * HD] for a in arrays) for h in range(count)]


def gathered(own_ref, low_ref, high_ref, all_ref):
    count = all_ref.shape[0]
    at = lax.axis_index("run")
    all_ref[at] = own_ref[...]
    all_ref[lax.rem(at + count - 1, count)] = low_ref[...]
    all_ref[lax.rem(at + 1, count)] = high_ref[...]


def fetches(sources, targets, sems):
    copies = []
    for n, (source, target) in enumerate(zip(sources, targets)):
        step = source.shape[0] // PIECES
        pieces = [
            pltpu.make_async_copy(source.at[pl.ds(i * step, step)], target.at[pl.ds(i * step, step)], sems.at[n, i])
            for i in range(PIECES)
        ]
        for piece in pieces:
            piece.start()
        copies.append(pieces)
    return copies


def arrive(pieces):
    for piece in pieces:
        piece.wait()


def forward_kernel(
    off_ref,
    own_ref,
    low_ref,
    high_ref,
    gain_ref,
    wq_hbm,
    wk_hbm,
    wv_hbm,
    wo_hbm,
    term_ref,
    dctx_ref,
    wq_ref,
    wk_ref,
    wv_ref,
    blocks,
    xs,
    gs,
    wo_ref,
    sems,
):
    wq_in, wk_in, wv_in, wo_in = fetches(
        (wq_hbm, wk_hbm, wv_hbm, wo_hbm), (wq_ref, wk_ref, wv_ref, wo_ref), sems
    )
    gathered(own_ref, low_ref, high_ref, blocks)
    runs, lines, rows, wide = blocks.shape
    parts = runs * lines
    share = wide // 2
    half = rows // 2
    width = parts * share
    squares = jnp.zeros((rows, wide), F32)
    for u in range(parts // 2):
        a = blocks[(2 * u) % runs, (2 * u) // runs]
        b = blocks[(2 * u + 1) % runs, (2 * u + 1) // runs]
        span = slice(wide * u, wide * (u + 1))
        x = jnp.concatenate([a[:, :share], b[:, :share]], axis=1)
        xs[:, span] = x
        gs[:, span] = jnp.concatenate([a[:, share:], b[:, share:]], axis=1)
        x = x.astype(F32)
        squares = squares + x * x
    inverse = lax.rsqrt(jnp.sum(squares, axis=1, keepdims=True) * (1.0 / width) + EPS)
    for u in range(parts // 2):
        span = slice(wide * u, wide * (u + 1))
        xs[:, span] = (xs[:, span].astype(F32) * inverse * gain_ref[:, span]).astype(BF16)
    normed = xs[...]
    arrive(wq_in)
    queries = dot(normed, wq_ref[...]).astype(BF16)
    arrive(wk_in)
    keys = dot(normed, wk_ref[...]).astype(BF16)
    arrive(wv_in)
    values = dot(normed, wv_ref[...]).astype(BF16)
    mask = causal(off_ref, 0, rows)
    context = jnp.concatenate(
        [dot(softmax(q, k, mask).astype(BF16), v) for q, k, v in heads_of(queries, keys, values)], axis=1
    ).astype(BF16)
    arrive(wo_in)
    for u in range(parts // 2):
        span = slice(wide * u, wide * (u + 1))
        out = dot(context, wo_ref[:, span]).astype(BF16)
        term_ref[2 * u] = jnp.concatenate([out[:half, :share], out[half:, :share]], axis=1)
        term_ref[2 * u + 1] = jnp.concatenate([out[:half, share:], out[half:, share:]], axis=1)
    dctx_ref[...] = dot_t(gs[...], wo_ref[...]).astype(BF16)


def backward_kernel(
    off_ref,
    own_ref,
    low_ref,
    high_ref,
    dctx_ref,
    gain_ref,
    wq_ref,
    wk_ref,
    wv_ref,
    term_ref,
    blocks,
    xs,
    ns,
    ds,
):
    gathered(own_ref, low_ref, high_ref, blocks)
    runs, lines, half, wide = blocks.shape
    parts = runs * lines
    share = wide // 2
    rows = half * 2
    width = parts * share
    squares = jnp.zeros((rows, wide), F32)
    for u in range(parts // 2):
        a = blocks[(2 * u) % runs, (2 * u) // runs]
        b = blocks[(2 * u + 1) % runs, (2 * u + 1) // runs]
        span = slice(wide * u, wide * (u + 1))
        x = jnp.concatenate(
            [
                jnp.concatenate([a[:, :share], b[:, :share]], axis=1),
                jnp.concatenate([a[:, share:], b[:, share:]], axis=1),
            ],
            axis=0,
        )
        xs[:, span] = x
        x = x.astype(F32)
        squares = squares + x * x
    inverse = lax.rsqrt(jnp.sum(squares, axis=1, keepdims=True) * (1.0 / width) + EPS)
    for u in range(parts // 2):
        span = slice(wide * u, wide * (u + 1))
        ns[:, span] = (xs[:, span].astype(F32) * inverse * gain_ref[:, span]).astype(BF16)
    normed = ns[...]
    queries = dot(normed, wq_ref[...]).astype(BF16)
    keys = dot(normed, wk_ref[...]).astype(BF16)
    values = dot(normed, wv_ref[...]).astype(BF16)
    mask = causal(off_ref, 1, rows)
    grads = []
    for q, k, v, dc in heads_of(queries, keys, values, dctx_ref[...]):
        weights = softmax(q, k, mask)
        dvalue = dot_tl(weights.astype(BF16), dc)
        dweights = dot_t(dc, v).astype(BF16).astype(F32)
        dscores = weights * (dweights - jnp.sum(dweights * weights, axis=1, keepdims=True))
        dscores = jnp.where(mask, dscores, 0.0) * (1.0 / math.sqrt(HD))
        dscores = dscores.astype(BF16)
        grads.append((dot(dscores, k), dot_tl(dscores, q), dvalue))
    dq, dk, dv = (jnp.concatenate(g, axis=1).astype(BF16) for g in zip(*grads))
    along = jnp.zeros((rows, wide), F32)
    for u in range(parts // 2):
        span = slice(wide * u, wide * (u + 1))
        grown = dot_t(dq, wq_ref[span, :]) + dot_t(dk, wk_ref[span, :]) + dot_t(dv, wv_ref[span, :])
        grown = grown * gain_ref[:, span]
        ds[:, span] = grown
        along = along + grown * xs[:, span].astype(F32)
    factor = jnp.sum(along, axis=1, keepdims=True) * (inverse * inverse * inverse) * (1.0 / width)
    for u in range(parts // 2):
        span = slice(wide * u, wide * (u + 1))
        out = (ds[:, span] * inverse - xs[:, span].astype(F32) * factor).astype(BF16)
        term_ref[2 * u] = jnp.concatenate([out[:half, :share], out[half:, :share]], axis=1)
        term_ref[2 * u + 1] = jnp.concatenate([out[:half, share:], out[half:, share:]], axis=1)


def kernel_call(body, outs, scratch, offsets, args, weights=()):
    vmem = pl.BlockSpec(memory_space=pltpu.VMEM)
    specs = [pl.BlockSpec(memory_space=pltpu.SMEM)] + [vmem] * len(args)
    specs += [pl.BlockSpec(memory_space=pltpu.HBM)] * len(weights)
    return pl.pallas_call(
        body,
        out_shape=outs,
        in_specs=specs,
        out_specs=tuple(vmem for _ in outs),
        scratch_shapes=scratch,
        compiler_params=pltpu.CompilerParams(vmem_limit_bytes=VMEM_LIMIT),
    )(offsets, *args, *[pltpu.with_memory_space_constraint(w, pltpu.HBM) for w in weights])


PIECES = 2
VMEM_LIMIT = 16 * 2**20


def forward_term(offsets, blocks, gain, wq, wk, wv, wo):
    lines, rows, wide = blocks[0].shape
    width = gain.shape[1]
    runs = len(blocks)
    outs = (
        jax.ShapeDtypeStruct((runs * lines, rows // 2, wide), BF16),
        jax.ShapeDtypeStruct((rows, wo.shape[0]), BF16),
        *[pltpu.VMEM(w.shape, w.dtype) for w in (wq, wk, wv)],
    )
    scratch = [
        pltpu.VMEM((runs, lines, rows, wide), BF16),
        pltpu.VMEM((rows, width), BF16),
        pltpu.VMEM((rows, width), BF16),
        pltpu.VMEM(wo.shape, wo.dtype),
        pltpu.SemaphoreType.DMA((4, PIECES)),
    ]
    return kernel_call(forward_kernel, outs, scratch, offsets, (*blocks, gain), (wq, wk, wv, wo))


def backward_term(offsets, blocks, dctx, gain, wq, wk, wv):
    lines, half, wide = blocks[0].shape
    width = gain.shape[1]
    runs = len(blocks)
    outs = (jax.ShapeDtypeStruct((runs * lines, half, wide), BF16),)
    scratch = [
        pltpu.VMEM((runs, lines, half, wide), BF16),
        pltpu.VMEM((2 * half, width), BF16),
        pltpu.VMEM((2 * half, width), BF16),
        pltpu.VMEM((2 * half, width), F32),
    ]
    return kernel_call(backward_kernel, outs, scratch, offsets, (*blocks, dctx, gain, wq, wk, wv))[0]


def folded(block):
    half = block.shape[0] // 2
    return jnp.concatenate([block[:half], block[half:]], axis=1)


def unfolded(block):
    share = block.shape[1] // 2
    return jnp.concatenate([block[:, :share], block[:, share:]], axis=0)


SECTION = ("x", "far", "core")
TENSOR = ("line", "run")
RUN = 3


def passed_along(block, distance):
    devices = range(lax.axis_size(SECTION))
    route = [(i - distance, i) for i in devices if i - distance in devices]
    return lax.ppermute(block, SECTION, route)


def around(block, axis, distance):
    count = lax.axis_size(axis)
    return lax.ppermute(block, axis, [(i, (i + distance) % count) for i in range(count)])


def mirrored(values, mask):
    section_count = lax.axis_size(SECTION)
    half = section_count // 2

    def swap_by(distance):
        route = [(i, i ^ distance) for i in range(section_count)]
        return lambda held: lax.ppermute(held, SECTION, route)

    return lax.switch(mask - half, [swap_by(half + i) for i in range(half)], values)


def exchanged(blocks, axes):
    return lax.all_to_all(blocks, axes, 0, 0, tiled=True)


def spread(block):
    own = exchanged(jnp.broadcast_to(block[None], (lax.axis_size("line"),) + block.shape), "line")
    return own, around(own, "run", 1), around(own, "run", -1)


def total(rows, terms):
    summed = jnp.sum(exchanged(terms, TENSOR).astype(F32), axis=0)
    return unfolded((folded(rows).astype(F32) + summed).astype(BF16))


def local(fwd_input, bwd_grad, parked, norm_gain, w_query, w_key, w_value, w_out, offsets, mirror):
    fwd_rows = fwd_input[0]
    grad_rows = bwd_grad[0]
    half = fwd_rows.shape[0] // 2
    pair = spread(jnp.concatenate([fwd_rows, grad_rows], axis=1))
    swapped = mirrored(jnp.concatenate([folded(fwd_rows), folded(parked[0])], axis=0), mirror[0])
    back = spread(swapped[half:])
    parked_rows = unfolded(swapped[:half])
    term, dctx, wq, wk, wv = forward_term(offsets, pair, norm_gain, w_query[0], w_key[0], w_value[0], w_out[0])
    layer_out = total(fwd_rows, term)
    next_rows = passed_along(layer_out, 1)
    back_term = backward_term(offsets, back, dctx, norm_gain, wq, wk, wv)
    grad_out = total(grad_rows, back_term)
    prev_rows = passed_along(grad_out, -1)
    return (next_rows[None], prev_rows[None], parked_rows[None])


def finer(mesh):
    tensor = mesh.shape["tensor"]
    x = math.isqrt(mesh.shape["section"] // 2)
    shape = (x, mesh.shape["section"] // 2 // x, 2, tensor // RUN, RUN)
    return Mesh(mesh.devices.reshape(shape), SECTION + TENSOR)


def solution(mesh):
    in_specs = (
        P(SECTION, None, TENSOR),
        P(SECTION, None, TENSOR),
        P(SECTION, None, TENSOR),
        P(SECTION, None),
        P(SECTION, None, TENSOR),
        P(SECTION, None, TENSOR),
        P(SECTION, None, TENSOR),
        P(SECTION, TENSOR, None),
        P(SECTION, None, None),
        P(),
    )
    out_specs = (
        P(SECTION, None, TENSOR),
        P(SECTION, None, TENSOR),
        P(SECTION, None, TENSOR),
    )
    return jax.shard_map(local, mesh=finer(mesh), in_specs=in_specs, out_specs=out_specs, check_vma=False)
```
